32 devices in a mesh: groups: 2 (over y), blk: 16 (over z, x, core).
Axes of the slice: x: 2, y: 2, z: 4, core: 2. Of those that a mesh axis runs over, the one named last changes fastest.
Arguments:
- queries: bfloat16 [96, 8192], P(('groups', 'blk')), parts along dimension 0, may hold values from -6 to 6
- new_kv: bfloat16 [96, 2, 1024], P(('groups', 'blk')), parts along dimension 0, may hold values from -6 to 6
- cache_kv: bfloat16 [96, 2, 256, 1024], P(('groups', 'blk')), parts along dimension 0, may hold values from -6 to 6
- parents: int32 [96], P(('groups', 'blk')), parts along dimension 0, may hold values from 0 to 47, as said below
- residual: bfloat16 [8192, 96], P('blk', 'groups'), parts along dimension 1, may hold values from -6 to 6
- out_proj: bfloat16 [8192, 8192], P('blk'), may hold values from -0.0625 to 0.0625
- norm_gain: bfloat16 [8192], P('blk'), may hold values from 0.099609375 to 1.8984375
- w_gate: bfloat16 [20480, 8192], P('blk'), may hold values from -0.0625 to 0.0625
- w_up: bfloat16 [20480, 8192], P('blk'), may hold values from -0.0625 to 0.0625
- w_down: bfloat16 [8192, 20480], P(None, 'blk'), may hold values from -0.0625 to 0.0625
Outputs:
- after_attention: bfloat16 [8192, 96], P('blk', 'groups'), parts along dimension 1
- layer_out: bfloat16 [8192, 96], P('blk', 'groups'), parts along dimension 1
The draws below stay inside these ranges and needn't reach their ends.
There are 2 independent parts, one for each index of `groups`. The reference program is written for one: setup_inputs(seed, part) draws one part's arguments, and reference() takes and returns one part's arrays. A program takes and returns all parts, laid end to end along the dimension named above; an argument that names none is the same for every part. Nothing has to cross between parts.
Inputs may be any that keep to these rules, and one draw needn't show every extreme that they name: Rows and parents count from 0 within each part, and parents[r] lies among the 3 rows of r's own aligned block, from 3 * (r // 3) on.
All inputs are finite; a program needn't handle non-finite values.
Results may differ from the reference program's by a relative error of at most 0.012.
Values may be sent and summed in bfloat16 or wider, within the bound.
A program may use at most 128 MiB of HBM per device.

```python
import math
import jax
import jax.numpy as jnp
from jax import lax

D = 8192
HQ = 64
KVH = 8
HD = 128
FF = 20480
CACHE = 256
R_DEV = 3
ROWS = 48


def common_parts(key):
    base_key = jax.random.fold_in(key, 11)
    query_base = jnp.clip(jax.random.normal(jax.random.fold_in(base_key, 1), (ROWS, HQ * HD), jnp.float32), -6.0, 6.0)
    return query_base


def draw_queries(key, part):
    query_base = common_parts(key)
    return query_base.astype(jnp.bfloat16)


def draw_new_kv(key, part):
    query_base = common_parts(key)
    query_sum = query_base.reshape(ROWS, KVH, HQ // KVH, HD).sum(axis=2).reshape(ROWS, KVH * HD)
    fresh_noise = jax.random.normal(jax.random.fold_in(key, 21), (ROWS, 2, KVH * HD), jnp.float32)
    new_key = jnp.clip(0.6 * fresh_noise[:, 0] + 0.35 * query_sum, -6.0, 6.0)
    new_value = jnp.clip(fresh_noise[:, 1], -6.0, 6.0)
    return jnp.stack([new_key, new_value], axis=1).astype(jnp.bfloat16)


def draw_cache_kv(key, part):
    fresh_noise = jnp.clip(jax.random.normal(jax.random.fold_in(key, 31), (ROWS, 2, CACHE, KVH * HD), jnp.float32), -6.0, 6.0)
    return fresh_noise.astype(jnp.bfloat16)


def draw_parents(key, part):
    offsets = jax.random.randint(jax.random.fold_in(key, 41), (ROWS,), 0, R_DEV)
    row_ids = jnp.arange(ROWS)
    offsets = jnp.where(row_ids == 0, 0, offsets)
    offsets = jnp.where(row_ids == ROWS - 1, R_DEV - 1, offsets)
    return (row_ids // R_DEV * R_DEV + offsets).astype(jnp.int32)


def strengthened(values, key, source, target, shards_of, factor):
    owner, partner = [(jnp.arange(values.shape[position]) // (values.shape[position] // shards_of)).reshape([-1 if axis == position else 1 for axis in range(values.ndim)]) for position in (source, target)]
    chosen = jax.random.permutation(key, shards_of)[partner]
    strong = (owner == chosen) | (owner == (partner + shards_of // 2) % shards_of)
    return jnp.where(strong, factor * values, values)


def steps_of(key, shape, pieces, least, largest):
    loudness = 1.0
    for dim, shards_of in pieces:
        heights = jax.random.uniform(jax.random.fold_in(jax.random.fold_in(key, 6), dim), (shards_of,), jnp.float32, least / len(pieces), largest / len(pieces))
        loudness = loudness * jnp.repeat(jnp.exp(heights), shape[dim] // shards_of).reshape((-1,) + (1,) * (len(shape) - 1 - dim))
    return loudness


def normal_values(own_key, extent, width, bound, pieces=(), held_as=jnp.bfloat16):
    level = steps_of(own_key, extent, pieces, -0.22, 0.18) if pieces else 1.0
    drawn = jax.random.normal(own_key, extent, jnp.float32) * width * level
    return jnp.minimum(jnp.maximum(drawn, -bound), bound).astype(held_as)


def heavy_noise(rng, shape, scale, reach, pieces, heavy, kind=jnp.bfloat16):
    entries = scale * jax.random.normal(rng, shape, jnp.float32)
    if pieces:
        entries = entries * steps_of(rng, shape, pieces, -0.22, 0.18)
    return jnp.clip(strengthened(entries, jax.random.fold_in(rng, 3), *heavy), -reach, reach).astype(kind)


def setup_inputs(seed: int = 0, part: int = 0) -> dict:
    key_list = jax.random.split(jax.random.key(seed), 11)
    part_splits = jax.random.split(jax.random.fold_in(key_list[10], part), 11)
    return {
        "queries": draw_queries(jax.random.fold_in(jax.random.fold_in(key_list[10], part), 71), part),
        "new_kv": draw_new_kv(jax.random.fold_in(jax.random.fold_in(key_list[10], part), 71), part),
        "cache_kv": draw_cache_kv(jax.random.fold_in(jax.random.fold_in(key_list[10], part), 71), part),
        "parents": draw_parents(jax.random.fold_in(jax.random.fold_in(key_list[10], part), 71), part),
        "residual": normal_values(part_splits[4], (D, ROWS), 1.0, 6.0, ((0, 16),)),
        "out_proj": normal_values(key_list[5], (D, HQ * HD), (HQ * HD) ** -0.5, 0.0625, ((0, 16),)),
        "norm_gain": jnp.clip(1.0 + 0.18 * jax.random.normal(key_list[6], (D,), jnp.float32), 0.099609375, 1.8984375).astype(jnp.bfloat16),
        "w_gate": normal_values(key_list[7], (FF, D), D ** -0.5, 0.0625, ((0, 16),)),
        "w_up": normal_values(key_list[8], (FF, D), D ** -0.5, 0.0625, ((0, 16),)),
        "w_down": heavy_noise(key_list[9], (D, FF), FF ** -0.5, 0.0625, ((1, 16),), (1, 0, 16, 2.0)),
    }


def one_row(cache_kv, operands):
    query_row, new_row, parent_row = operands
    group_size = HQ // KVH
    picked = cache_kv[parent_row]
    key_all = jnp.concatenate([picked[0], new_row[0][None, :]], axis=0).reshape(CACHE + 1, KVH, HD)
    value_all = jnp.concatenate([picked[1], new_row[1][None, :]], axis=0).reshape(CACHE + 1, KVH, HD)
    query_heads = query_row.reshape(KVH, group_size, HD)
    score_all = jnp.einsum('gjd,cgd->gjc', query_heads.astype(jnp.float32), key_all.astype(jnp.float32)) * (1.0 / math.sqrt(HD))
    score_top = lax.optimization_barrier(jnp.max(score_all, axis=-1, keepdims=True))
    expo = jnp.exp(score_all - score_top)
    weights = (expo / lax.optimization_barrier(jnp.sum(expo, axis=-1, keepdims=True))).astype(jnp.bfloat16)
    mixed_heads = jnp.einsum('gjc,cgd->gjd', weights.astype(jnp.float32), value_all.astype(jnp.float32))
    return mixed_heads.reshape(HQ * HD).astype(jnp.bfloat16)

def reference(queries, new_kv, cache_kv, parents, residual, out_proj, norm_gain, w_gate, w_up, w_down):
    attended = lax.map(lambda operands: one_row(cache_kv, operands), (queries, new_kv, parents.astype(jnp.int32)))
    projected = jnp.dot(out_proj, attended.T, preferred_element_type=jnp.float32)
    after_attention = (residual.astype(jnp.float32) + projected).astype(jnp.bfloat16)
    widened = after_attention.astype(jnp.float32)
    inverse_rms = lax.rsqrt(lax.optimization_barrier(jnp.sum(widened * widened, axis=0)) / D + 1e-06)
    normed = (widened * inverse_rms[None, :] * norm_gain.astype(jnp.float32)[:, None]).astype(jnp.bfloat16)
    gate_sum = jnp.dot(w_gate, normed, preferred_element_type=jnp.float32)
    up_sum = jnp.dot(w_up, normed, preferred_element_type=jnp.float32)
    hidden = (jax.nn.silu(gate_sum) * up_sum).astype(jnp.bfloat16)
    ffn_delta = jnp.dot(w_down, hidden, preferred_element_type=jnp.float32)
    layer_out = (widened + ffn_delta).astype(jnp.bfloat16)
    return (after_attention, layer_out)
```

```python
import functools
import math

import jax
import jax.numpy as jnp
from jax import lax
from jax.experimental import pallas as pl
from jax.experimental.pallas import tpu as pltpu
from jax.sharding import PartitionSpec as P

D = 8192
HQ = 64
KVH = 8
HD = 128
CACHE = 256


epsilon = 1e-06


def attend_rows(queries, new_kv, cache_kv, parents):
    row_count = queries.shape[0]
    group_size = HQ // KVH
    local_parent = parents - lax.axis_index("blk") * row_count
    chosen = jnp.broadcast_to(cache_kv[0], cache_kv.shape)
    for i in range(1, row_count):
        here = (local_parent == i)[:, None, None, None]
        chosen = jnp.where(here, cache_kv[i], chosen)
    cache_keys = chosen[:, 0].reshape(row_count, CACHE, KVH, HD)
    cache_values = chosen[:, 1].reshape(row_count, CACHE, KVH, HD)
    new_key = new_kv[:, 0].reshape(row_count, KVH, HD)
    new_value = new_kv[:, 1].reshape(row_count, KVH, HD)
    query_heads = queries.reshape(row_count, KVH, group_size, HD)
    score_scale = 1.0 / math.sqrt(HD)
    score_cache = (
        jnp.einsum("rgjd,rcgd->rgjc", query_heads, cache_keys, preferred_element_type=jnp.float32)
        * score_scale
    )
    score_new = (
        jnp.einsum("rgjd,rgd->rgj", query_heads, new_key, preferred_element_type=jnp.float32)
        * score_scale
    )
    score_top = jnp.maximum(jnp.max(score_cache, axis=-1), score_new)
    expo_cache = jnp.exp(score_cache - score_top[..., None])
    expo_new = jnp.exp(score_new - score_top)
    denom_sum = jnp.sum(expo_cache, axis=-1) + expo_new
    weight_cache = (expo_cache / denom_sum[..., None]).astype(jnp.bfloat16)
    weight_new = (expo_new / denom_sum).astype(jnp.bfloat16)
    mixed_heads = jnp.einsum(
        "rgjc,rcgd->rgjd", weight_cache, cache_values, preferred_element_type=jnp.float32
    )
    mixed_heads = (
        mixed_heads
        + weight_new.astype(jnp.float32)[..., None] * new_value.astype(jnp.float32)[:, :, None, :]
    )
    return mixed_heads.reshape(row_count, HQ * HD).astype(jnp.bfloat16)


def shards(queries, new_kv, cache_kv, parents, residual, out_proj, norm_gain, w_gate, w_up, w_down):
    attended = attend_rows(queries, new_kv, cache_kv, parents)
    projected = lax.dot_general(
        out_proj,
        lax.all_gather(attended, "blk", axis=0, tiled=True),
        (((1,), (1,)), ((), ())),
        preferred_element_type=jnp.float32,
    )
    after_attention = (residual.astype(jnp.float32) + projected).astype(jnp.bfloat16)
    widened = after_attention.astype(jnp.float32)
    gathered, gain_all = (
        lax.all_gather(after_attention, "blk", axis=0, tiled=True),
        lax.all_gather(norm_gain, "blk", axis=0, tiled=True),
    )
    gathered_wide = gathered.astype(jnp.float32)
    inverse_rms = lax.rsqrt(jnp.sum(gathered_wide * gathered_wide, axis=0) / D + epsilon)
    normed_all = (
        gathered_wide * inverse_rms[None, :] * gain_all.astype(jnp.float32)[:, None]
    ).astype(jnp.bfloat16)
    gate_sum = jnp.dot(w_gate, normed_all, preferred_element_type=jnp.float32)
    up_sum = jnp.dot(w_up, normed_all, preferred_element_type=jnp.float32)
    hidden = (jax.nn.silu(gate_sum) * up_sum).astype(jnp.bfloat16)
    ffn_delta = lax.psum_scatter(
        jnp.dot(w_down, hidden, preferred_element_type=jnp.float32),
        "blk",
        scatter_dimension=0,
        tiled=True,
    )
    layer_out = (widened + ffn_delta).astype(jnp.bfloat16)
    return (after_attention, layer_out)


LANES = 128
TILE = 256
NZ, NX, NC = 4, 2, 2
SPARE = 3
MESH_IDS = pl.DeviceIdType.MESH
NT = (((1,), (1,)), ((), ()))


def push(tile, step, unit):
    if step % 2:
        pltpu.matmul_push_rhs(tile.T, 1, unit)
    else:
        pltpu.matmul_push_rhs(tile, 0, unit, transpose=True)


def times_transposed(parts, weights, accs):
    for k, part in enumerate(parts):
        for unit, acc in enumerate(accs):
            push(weights[unit * TILE : (unit + 1) * TILE, k * TILE : (k + 1) * TILE], k, unit)
            pltpu.matmul_acc_lhs(acc, part, k % 2)
    return jnp.concatenate([pltpu.matmul_pop(acc) for acc in accs], axis=1)


def fused_kernel(
    rows,
    parents_ref,
    queries_ref,
    new_kv_ref,
    gain_ref,
    residual_ref,
    cache_hbm,
    proj_hbm,
    gate_hbm,
    up_hbm,
    down_hbm,
    after_ref,
    out_ref,
    cache,
    proj_w,
    gate_w,
    up_w,
    down_w,
    att_slots,
    att_wide,
    head_rows,
    own_rows,
    act_slots,
    squares,
    rs_send,
    core_recv,
    x_recv,
    z_recv,
    cache_sem,
    proj_sem,
    gate_sem,
    up_sem,
    down_sem,
    square_send,
    square_recv,
    ag1_send,
    ag1_recv,
    ag2_send,
    ag2_recv,
    own_send,
    core_sem,
    x_sem,
    z_sem,
):
    me = lax.axis_index("blk")
    core = lax.rem(me, NC)
    along_x = lax.rem(lax.div(me, NC), NX)
    along_z = lax.div(me, NC * NX)
    n = NZ * NX * NC
    width = proj_hbm.shape[0]
    hidden_width = gate_hbm.shape[0]
    total_rows = n * rows

    z_places = (
        along_z,
        along_z + 1 - 2 * lax.rem(along_z, 2),
        NZ - 1 - along_z,
        lax.rem(along_z + 2, NZ),
    )

    def pick(values, t):
        chosen = jnp.int32(values[-1])
        for i in range(len(values) - 1):
            chosen = jnp.where(t == i, values[i], chosen)
        return chosen

    def rank_of(q, dx, dc):
        return (
            z_places[q] * (NX * NC)
            + lax.rem(along_x + dx, NX) * NC
            + lax.rem(core + dc, NC)
        )

    x_peer = rank_of(0, 1, 0)
    core_peer = rank_of(0, 0, 1)

    arrivals = [(0, 0, 0), (0, 0, 1)]
    for q in range(1, NZ):
        arrivals += [(q, 0, 0), (q - 1, 1, 0), (q - 1, 1, 1), (q, 0, 1)]
    arrivals += [(NZ - 1, 1, 0), (NZ - 1, 1, 1)]

    def ordered(t):
        return pick([rank_of(*arrival) for arrival in arrivals], t)

    barrier = pltpu.get_barrier_semaphore()
    z_peers = [rank_of(q, 0, 0) for q in range(1, NZ)]
    peers = [core_peer, x_peer] + z_peers
    for peer in peers:
        pl.semaphore_signal(
            barrier, inc=1, device_id={"blk": peer}, device_id_type=MESH_IDS
        )

    def cache_copy(r):
        return pltpu.make_async_copy(cache_hbm.at[r], cache.at[r], cache_sem.at[r])

    def proj_copy(i):
        part = proj_hbm.shape[1] // 4
        span = pl.ds(i * part, part)
        return pltpu.make_async_copy(
            proj_hbm.at[:, span], proj_w.at[:, span], proj_sem.at[i]
        )

    def slab(s):
        return pl.ds(pl.multiple_of(s * width, width), width)

    def gate_copy(t):
        span = slab(ordered(t))
        return pltpu.make_async_copy(
            gate_hbm.at[:, span], gate_w.at[:, span], gate_sem.at[t]
        )

    def up_copy(t):
        span = slab(ordered(t))
        return pltpu.make_async_copy(
            up_hbm.at[:, span], up_w.at[:, span], up_sem.at[t]
        )

    per_row = proj_hbm.shape[1] // hidden_width

    def down_place(t):
        if t < SPARE:
            return down_w.at[t]
        t -= SPARE
        if t < per_row:
            return proj_w.at[:, pl.ds(t * hidden_width, hidden_width)]
        t -= per_row
        return gate_w.at[
            pl.ds(t // per_row * width, width),
            pl.ds(t % per_row * hidden_width, hidden_width),
        ]

    def down_owner(t):
        k, group = t % NZ, t // NZ
        return rank_of(NZ - 1 - k, 1 - group // 2, 1 - group % 2)

    def down_copy(t):
        return pltpu.make_async_copy(
            down_hbm.at[slab(down_owner(t)), :], down_place(t), down_sem.at[t]
        )

    for r in range(rows):
        cache_copy(r).start()
    for i in range(4):
        proj_copy(i).start()

    def start_weights(t, carry):
        gate_copy(t).start()
        up_copy(t).start()
        return carry

    lax.fori_loop(0, n, start_weights, 0)
    for t in range(SPARE):
        down_copy(t).start()

    query_wide = queries_ref[...].astype(jnp.float32)
    for h in range(HQ):
        head_rows[pl.ds(h, rows, stride=HQ), :] = query_wide[:, h * HD : (h + 1) * HD]
    group_size = HQ // KVH
    pair = 2 * group_size
    own_head = lax.broadcasted_iota(jnp.int32, (pair, TILE), 0) // group_size == (
        lax.broadcasted_iota(jnp.int32, (pair, TILE), 1) // HD
    )
    score_scale = 1.0 / math.sqrt(HD)
    for r in range(rows):
        cache_copy(r).wait()

    def attend(*accs):
        pairs = range(KVH // 2)
        for r in range(rows):
            parent = lax.rem(parents_ref[r], rows)
            spreads, news = [], []
            for p in pairs:
                unit, step = p % 2, p // 2
                span = slice(p * TILE, (p + 1) * TILE)
                head_block = head_rows[r * HQ + p * pair : r * HQ + (p + 1) * pair, :]
                spread = jnp.where(own_head, jnp.concatenate([head_block] * 2, axis=1), 0.0)
                push(cache[parent, 0, :, span], step, unit)
                pltpu.matmul_acc_lhs(accs[p], spread.astype(jnp.bfloat16), step)
                new_key = new_kv_ref[r, 0:1, span].astype(jnp.float32)
                news.append(jnp.sum(spread * new_key, axis=1, keepdims=True))
            scores = jnp.concatenate([pltpu.matmul_pop(accs[p]) for p in pairs], axis=0) * score_scale
            score_new = jnp.concatenate(news, axis=0) * score_scale
            top = jnp.maximum(jnp.max(scores, axis=1, keepdims=True), score_new)
            expo = jnp.exp(scores - top)
            expo_new = jnp.exp(score_new - top)
            denom = jnp.sum(expo, axis=1, keepdims=True) + expo_new
            weights = (expo / denom).astype(jnp.bfloat16)
            weight_new = (expo_new / denom).astype(jnp.bfloat16).astype(jnp.float32)
            for p in pairs:
                unit, step = p % 2, p // 2
                span = slice(p * TILE, (p + 1) * TILE)
                own = slice(p * pair, (p + 1) * pair)
                pltpu.matmul_push_rhs(cache[parent, 1, :, span], step, unit)
                pltpu.matmul_acc_lhs(accs[p], weights[own], step)
            for p in pairs:
                span = slice(p * TILE, (p + 1) * TILE)
                new_value = new_kv_ref[r, 1:2, span].astype(jnp.float32)
                mixed = pltpu.matmul_pop(accs[p]) + weight_new[p * pair : (p + 1) * pair] * new_value
                for i in range(2):
                    head_rows[pl.ds(r * HQ + p * pair + i * group_size, group_size), :] = mixed[
                        i * group_size : (i + 1) * group_size, i * HD : (i + 1) * HD
                    ]

    pl.run_scoped(attend, *[pltpu.ACC(p % 2)((pair, TILE), jnp.float32) for p in range(KVH // 2)])
    lines = rows * KVH
    for j in range(group_size):
        own_rows[:, j * HD : (j + 1) * HD] = head_rows[
            pl.ds(j, lines, stride=group_size), :
        ]
    att_slots[me] = own_rows[...].astype(jnp.bfloat16)
    pl.semaphore_wait(barrier, len(peers))

    def gather_ops(slots, send_sem, recv_sem):
        def copy(s, k, device):
            return pltpu.make_async_remote_copy(
                src_ref=slots.at[s],
                dst_ref=slots.at[s],
                send_sem=send_sem.at[k],
                recv_sem=recv_sem.at[s],
                device_id={"blk": device},
                device_id_type=MESH_IDS,
            )

        def begin():
            copy(me, 7, core_peer).start()
            copy(me, 3, x_peer).start()
            for q in (3, 2, 1):
                copy(me, q - 1, rank_of(q, 0, 0)).start()

        def act(t):
            q, dx, dc = arrivals[t]
            s = rank_of(q, dx, dc)
            copy(s, 0, core_peer).wait_recv()
            if dc == 0 and dx == 0:
                copy(s, 3 + q, x_peer).start()
                copy(s, 7 + q, core_peer).start()
            elif dc == 0:
                copy(s, 11 + q, core_peer).start()

        def finish():
            for k in range(15):
                copy(me, k, core_peer).wait_send()

        return begin, act, finish

    begin, act, finish1 = gather_ops(att_slots, ag1_send, ag1_recv)
    begin()

    for t in range(1, n):
        act(t)

    def widen(s, carry):
        wide = att_slots[s].astype(jnp.float32)
        for j in range(group_size):
            att_wide[j, pl.ds(pl.multiple_of(s * lines, 8), lines), :] = wide[
                :, j * HD : (j + 1) * HD
            ]
        return carry

    lax.fori_loop(0, n, widen, 0)
    for i in range(4):
        proj_copy(i).wait()

    def project(*accs):
        parts = []
        for g in range(KVH):
            for j in range(0, group_size, 2):
                parts.append(
                    jnp.concatenate(
                        [
                            att_wide[j + i, pl.ds(g, total_rows, stride=KVH), :]
                            for i in range(2)
                        ],
                        axis=1,
                    ).astype(jnp.bfloat16)
                )
        return times_transposed(parts, proj_w, accs)

    acc_types = [pltpu.ACC(unit)((total_rows, TILE), jnp.float32) for unit in range(2)]
    projected = pl.run_scoped(project, *acc_types)
    after = (residual_ref[...].astype(jnp.float32) + projected).astype(jnp.bfloat16)
    wide = after.astype(jnp.float32)
    gain = gain_ref[...].astype(jnp.float32).reshape(1, width)
    act_slots[me] = (wide * gain).astype(jnp.bfloat16)
    begin, act, finish2 = gather_ops(act_slots, ag2_send, ag2_recv)
    begin()
    for t in range(SPARE, SPARE + per_row):
        down_copy(t).start()
    after_ref[...] = after

    folded = wide[:, 0:LANES] * wide[:, 0:LANES]
    for j in range(1, width // LANES):
        part = wide[:, j * LANES : (j + 1) * LANES]
        folded = folded + part * part
    squares[0] = folded

    def square_copy(k):
        slot = (0, 2, 4, 4, 4)[k]
        return pltpu.make_async_remote_copy(
            src_ref=squares.at[slot],
            dst_ref=squares.at[(1, 3, 5, 6, 7)[k]],
            send_sem=square_send.at[k],
            recv_sem=square_recv.at[k],
            device_id={"blk": peers[k]},
            device_id_type=MESH_IDS,
        )

    square_copy(0).start()

    def squares_over_cores():
        square_copy(0).wait_recv()
        squares[2] = squares[0] + squares[1]
        square_copy(1).start()

    def squares_over_x():
        square_copy(1).wait_recv()
        squares[4] = squares[2] + squares[3]
        for k in (2, 3, 4):
            square_copy(k).start()

    def feed_forward(*accs):
        gate_accs, up_accs = accs[0::2], accs[1::2]

        def consume(t, carry):
            s = ordered(t)
            for i in range(1, n):
                pl.when(t == i)(functools.partial(act, i))
            pl.when(t == 3)(squares_over_cores)
            pl.when(t == 7)(squares_over_x)
            gate_copy(t).wait()
            up_copy(t).wait()
            for k in range(width // TILE):
                part = act_slots[s, :, k * TILE : (k + 1) * TILE]
                span = pl.ds(pl.multiple_of(s * width + k * TILE, TILE), TILE)
                for i in range(hidden_width // TILE):
                    step = k * (hidden_width // TILE) + i
                    tall = pl.ds(i * TILE, TILE)
                    for unit, weights in enumerate((gate_w, up_w)):
                        push(weights[tall, span], step, unit)
                        pltpu.matmul_acc_lhs((gate_accs, up_accs)[unit][i], part, step % 2)
            return carry

        lax.fori_loop(0, n, consume, 0)
        total = squares[4]
        for k in (2, 3, 4):
            square_copy(k).wait_recv()
            total = total + squares[k + 3]
        inverse_rms = lax.rsqrt(
            jnp.sum(total, axis=1, keepdims=True) / (n * width) + epsilon
        )
        hidden = []
        for gate_acc, up_acc in zip(gate_accs, up_accs):
            gate_sum = pltpu.matmul_pop(gate_acc) * inverse_rms
            up_sum = pltpu.matmul_pop(up_acc) * inverse_rms
            hidden.append((gate_sum / (1.0 + jnp.exp(-gate_sum)) * up_sum).astype(jnp.bfloat16))
        return tuple(hidden)

    hidden = pl.run_scoped(feed_forward, *acc_types * (hidden_width // TILE))
    for t in range(SPARE + per_row, n):
        down_copy(t).start()
    def core_copy(t):
        i = t % NZ + t // (2 * NZ) * NZ
        return pltpu.make_async_remote_copy(
            src_ref=rs_send.at[t],
            dst_ref=core_recv.at[i],
            send_sem=own_send.at[t],
            recv_sem=core_sem.at[i],
            device_id={"blk": core_peer},
            device_id_type=MESH_IDS,
        )

    def x_copy(t):
        return pltpu.make_async_remote_copy(
            src_ref=rs_send.at[t],
            dst_ref=x_recv.at[t % NZ],
            send_sem=own_send.at[t],
            recv_sem=x_sem.at[t % NZ],
            device_id={"blk": x_peer},
            device_id_type=MESH_IDS,
        )

    def z_copy(t):
        return pltpu.make_async_remote_copy(
            src_ref=rs_send.at[t],
            dst_ref=z_recv.at[t % NZ],
            send_sem=own_send.at[t],
            recv_sem=z_sem.at[t % NZ],
            device_id={"blk": rank_of(NZ - 1 - t % NZ, 0, 0)},
            device_id_type=MESH_IDS,
        )

    def term(t):
        down_copy(t).wait()
        return pl.run_scoped(
            lambda *accs: times_transposed(hidden, down_place(t), accs), *acc_types
        )

    sends = []
    for t in (0, 1, 2, 4, 3, 5, 8, 6, 9, 7, 10, 11, 12, 13, 14):
        total = term(t)
        group = t // NZ
        if group % 2 == 1:
            core_copy(t - NZ).wait_recv()
            total = total + core_recv[t % NZ + group // 2 * NZ].astype(jnp.float32)
        if group == 3:
            x_copy(t - 2 * NZ).wait_recv()
            total = total + x_recv[t % NZ].astype(jnp.float32)
        rs_send[t] = total.astype(jnp.bfloat16)
        copy = (core_copy, x_copy, core_copy, z_copy)[group](t)
        copy.start()
        sends.append(copy)
    t = n - 1
    total = term(t)
    core_copy(t - NZ).wait_recv()
    total = total + core_recv[2 * NZ - 1].astype(jnp.float32)
    x_copy(t - 2 * NZ).wait_recv()
    total = total + x_recv[NZ - 1].astype(jnp.float32)
    total = total + after_ref[...].astype(jnp.float32)
    for k in range(NZ - 1):
        z_copy(n - NZ + k).wait_recv()
        total = total + z_recv[k].astype(jnp.float32)
    out_ref[...] = total.astype(jnp.bfloat16)
    for copy in sends:
        copy.wait_send()
    finish1()
    finish2()
    for k in range(len(peers)):
        square_copy(k).wait_send()


def hand_over(after_ref, out_ref, after_to, out_to):
    after_to[...] = after_ref[...]
    out_to[...] = out_ref[...]


def fused_shards(
    queries, new_kv, cache_kv, parents, residual, out_proj, norm_gain, w_gate, w_up, w_down
):
    rows = queries.shape[0]
    n = NZ * NX * NC
    width, depth = out_proj.shape
    hidden_width = w_gate.shape[0]
    total_rows = n * rows
    bf16, f32 = jnp.bfloat16, jnp.float32
    in_vmem = pl.BlockSpec(memory_space=pltpu.VMEM)
    outside = pl.BlockSpec(memory_space=pl.ANY)
    dma = pltpu.SemaphoreType.DMA
    after, out = pl.pallas_call(
        functools.partial(fused_kernel, rows),
        out_shape=(
            jax.ShapeDtypeStruct((total_rows, width), bf16),
            jax.ShapeDtypeStruct((total_rows, width), bf16),
        ),
        in_specs=[pl.BlockSpec(memory_space=pltpu.SMEM)] + [in_vmem] * 4 + [outside] * 5,
        out_specs=(in_vmem, in_vmem),
        scratch_shapes=[
            pltpu.VMEM(cache_kv.shape, bf16),
            pltpu.VMEM((width, depth), bf16),
            pltpu.VMEM((hidden_width, depth), bf16),
            pltpu.VMEM((hidden_width, depth), bf16),
            pltpu.VMEM((SPARE, width, hidden_width), bf16),
            pltpu.VMEM((n, rows * KVH, depth // KVH), bf16),
            pltpu.VMEM((HQ // KVH, total_rows * KVH, HD), f32),
            pltpu.VMEM((rows * HQ, HD), f32),
            pltpu.VMEM((rows * KVH, depth // KVH), f32),
            pltpu.VMEM((n, total_rows, width), bf16),
            pltpu.VMEM((8, total_rows, LANES), f32),
            pltpu.VMEM((n - 1, total_rows, width), bf16),
            pltpu.VMEM((NZ * NX, total_rows, width), bf16),
            pltpu.VMEM((NZ, total_rows, width), bf16),
            pltpu.VMEM((NZ - 1, total_rows, width), bf16),
            dma((rows,)),
            dma((4,)),
            dma((n,)),
            dma((n,)),
            dma((n,)),
            dma((5,)),
            dma((5,)),
            dma((n - 1,)),
            dma((n,)),
            dma((n - 1,)),
            dma((n,)),
            dma((n - 1,)),
            dma((NZ * NX,)),
            dma((NZ,)),
            dma((NZ - 1,)),
        ],
        compiler_params=pltpu.CompilerParams(
            collective_id=0, has_side_effects=True, vmem_limit_bytes=67043328
        ),
        name="layer",
    )(
        parents,
        queries,
        new_kv,
        norm_gain,
        residual.T,
        cache_kv,
        out_proj,
        w_gate,
        w_up,
        w_down,
    )
    after, out = pl.pallas_call(
        hand_over, out_shape=(after, out), in_specs=[in_vmem] * 2, out_specs=(in_vmem, in_vmem)
    )(after, out)
    return after.T, out.T


def solution(mesh):
    fits = mesh.shape["blk"] == NZ * NX * NC
    return jax.shard_map(
        fused_shards if fits else shards,
        mesh=mesh,
        in_specs=(
            P(("groups", "blk"), None),
            P(("groups", "blk"), None, None),
            P(("groups", "blk"), None, None, None),
            P(("groups", "blk")),
            P("blk", "groups"),
            P("blk", None),
            P("blk"),
            P("blk", None),
            P("blk", None),
            P(None, "blk"),
        ),
        out_specs=(P("blk", "groups"), P("blk", "groups")),
        check_vma=False,
    )
```

```python
import functools
import math

import jax
import jax.numpy as jnp
from jax import lax
from jax.experimental import pallas as pl
from jax.experimental.pallas import tpu as pltpu
from jax.sharding import PartitionSpec as P

D = 8192
HQ = 64
KVH = 8
HD = 128
CACHE = 256


epsilon = 1e-06


def attend_rows(queries, new_kv, cache_kv, parents):
    row_count = queries.shape[0]
    group_size = HQ // KVH
    local_parent = parents - lax.axis_index("blk") * row_count
    chosen = jnp.broadcast_to(cache_kv[0], cache_kv.shape)
    for i in range(1, row_count):
        here = (local_parent == i)[:, None, None, None]
        chosen = jnp.where(here, cache_kv[i], chosen)
    cache_keys = chosen[:, 0].reshape(row_count, CACHE, KVH, HD)
    cache_values = chosen[:, 1].reshape(row_count, CACHE, KVH, HD)
    new_key = new_kv[:, 0].reshape(row_count, KVH, HD)
    new_value = new_kv[:, 1].reshape(row_count, KVH, HD)
    query_heads = queries.reshape(row_count, KVH, group_size, HD)
    score_scale = 1.0 / math.sqrt(HD)
    score_cache = (
        jnp.einsum("rgjd,rcgd->rgjc", query_heads, cache_keys, preferred_element_type=jnp.float32)
        * score_scale
    )
    score_new = (
        jnp.einsum("rgjd,rgd->rgj", query_heads, new_key, preferred_element_type=jnp.float32)
        * score_scale
    )
    score_top = jnp.maximum(jnp.max(score_cache, axis=-1), score_new)
    expo_cache = jnp.exp(score_cache - score_top[..., None])
    expo_new = jnp.exp(score_new - score_top)
    denom_sum = jnp.sum(expo_cache, axis=-1) + expo_new
    weight_cache = (expo_cache / denom_sum[..., None]).astype(jnp.bfloat16)
    weight_new = (expo_new / denom_sum).astype(jnp.bfloat16)
    mixed_heads = jnp.einsum(
        "rgjc,rcgd->rgjd", weight_cache, cache_values, preferred_element_type=jnp.float32
    )
    mixed_heads = (
        mixed_heads
        + weight_new.astype(jnp.float32)[..., None] * new_value.astype(jnp.float32)[:, :, None, :]
    )
    return mixed_heads.reshape(row_count, HQ * HD).astype(jnp.bfloat16)


def shards(queries, new_kv, cache_kv, parents, residual, out_proj, norm_gain, w_gate, w_up, w_down):
    attended = attend_rows(queries, new_kv, cache_kv, parents)
    projected = lax.dot_general(
        out_proj,
        lax.all_gather(attended, "blk", axis=0, tiled=True),
        (((1,), (1,)), ((), ())),
        preferred_element_type=jnp.float32,
    )
    after_attention = (residual.astype(jnp.float32) + projected).astype(jnp.bfloat16)
    widened = after_attention.astype(jnp.float32)
    gathered, gain_all = (
        lax.all_gather(after_attention, "blk", axis=0, tiled=True),
        lax.all_gather(norm_gain, "blk", axis=0, tiled=True),
    )
    gathered_wide = gathered.astype(jnp.float32)
    inverse_rms = lax.rsqrt(jnp.sum(gathered_wide * gathered_wide, axis=0) / D + epsilon)
    normed_all = (
        gathered_wide * inverse_rms[None, :] * gain_all.astype(jnp.float32)[:, None]
    ).astype(jnp.bfloat16)
    gate_sum = jnp.dot(w_gate, normed_all, preferred_element_type=jnp.float32)
    up_sum = jnp.dot(w_up, normed_all, preferred_element_type=jnp.float32)
    hidden = (jax.nn.silu(gate_sum) * up_sum).astype(jnp.bfloat16)
    ffn_delta = lax.psum_scatter(
        jnp.dot(w_down, hidden, preferred_element_type=jnp.float32),
        "blk",
        scatter_dimension=0,
        tiled=True,
    )
    layer_out = (widened + ffn_delta).astype(jnp.bfloat16)
    return (after_attention, layer_out)


LANES = 128
TILE = 256
NZ, NX, NC = 4, 2, 2
SPARE = 3
MESH_IDS = pl.DeviceIdType.MESH
NT = (((1,), (1,)), ((), ()))


def push(tile, step, unit):
    if step % 2:
        pltpu.matmul_push_rhs(tile.T, 1, unit)
    else:
        pltpu.matmul_push_rhs(tile, 0, unit, transpose=True)


def times_transposed(parts, weights, accs):
    for k, part in enumerate(parts):
        for unit, acc in enumerate(accs):
            push(weights[unit * TILE : (unit + 1) * TILE, k * TILE : (k + 1) * TILE], k, unit)
            pltpu.matmul_acc_lhs(acc, part, k % 2)
    return jnp.concatenate([pltpu.matmul_pop(acc) for acc in accs], axis=1)


def fused_kernel(
    rows,
    parents_ref,
    queries_ref,
    new_kv_ref,
    gain_ref,
    residual_ref,
    cache_hbm,
    proj_hbm,
    gate_hbm,
    up_hbm,
    down_hbm,
    after_ref,
    out_ref,
    cache,
    proj_w,
    gate_w,
    up_w,
    down_w,
    att_slots,
    att_wide,
    head_rows,
    own_rows,
    act_slots,
    squares,
    rs_send,
    core_recv,
    x_recv,
    z_recv,
    cache_sem,
    proj_sem,
    gate_sem,
    up_sem,
    down_sem,
    square_send,
    square_recv,
    ag1_send,
    ag1_recv,
    ag2_send,
    ag2_recv,
    own_send,
    core_sem,
    x_sem,
    z_sem,
):
    me = lax.axis_index("blk")
    core = lax.rem(me, NC)
    along_x = lax.rem(lax.div(me, NC), NX)
    along_z = lax.div(me, NC * NX)
    n = NZ * NX * NC
    width = proj_hbm.shape[0]
    hidden_width = gate_hbm.shape[0]
    total_rows = n * rows

    z_places = (
        along_z,
        along_z + 1 - 2 * lax.rem(along_z, 2),
        NZ - 1 - along_z,
        lax.rem(along_z + 2, NZ),
    )

    def pick(values, t):
        chosen = jnp.int32(values[-1])
        for i in range(len(values) - 1):
            chosen = jnp.where(t == i, values[i], chosen)
        return chosen

    def rank_of(q, dx, dc):
        return (
            z_places[q] * (NX * NC)
            + lax.rem(along_x + dx, NX) * NC
            + lax.rem(core + dc, NC)
        )

    x_peer = rank_of(0, 1, 0)
    core_peer = rank_of(0, 0, 1)

    own, over_x = [(q, 0, 0) for q in range(NZ)], [(q, 1, 0) for q in range(NZ)]
    arrivals = [(0, 0, 0), (0, 0, 1), (1, 0, 0), (0, 1, 0), (0, 1, 1), (1, 0, 1)]
    arrivals += [(2, 0, 0), (3, 0, 0), (2, 0, 1), (3, 0, 1), (1, 1, 0), (1, 1, 1)]
    arrivals += [(2, 1, 0), (3, 1, 0), (2, 1, 1), (3, 1, 1)]
    awaited = {1: [(0, 0, 1)], 2: [(1, 0, 0)], 3: [(0, 1, 0)], 4: [(0, 1, 1)]}
    awaited[5] = [(2, 0, 0), (3, 0, 0), (1, 0, 1)]
    awaited[8] = [(1, 1, 0), (2, 0, 1)]
    awaited[9] = [(3, 0, 1)]
    awaited[11] = [(1, 1, 1)]
    awaited[12] = [(2, 1, 0), (3, 1, 0)]
    awaited[14] = [(2, 1, 1)]
    awaited[15] = [(3, 1, 1)]

    def ordered(t):
        return pick([rank_of(*arrival) for arrival in arrivals], t)

    barrier = pltpu.get_barrier_semaphore()
    z_peers = [rank_of(q, 0, 0) for q in range(1, NZ)]
    peers = [core_peer, x_peer] + z_peers
    for peer in peers:
        pl.semaphore_signal(
            barrier, inc=1, device_id={"blk": peer}, device_id_type=MESH_IDS
        )

    def cache_copy(r):
        return pltpu.make_async_copy(cache_hbm.at[r], cache.at[r], cache_sem.at[r])

    def proj_copy(i):
        part = proj_hbm.shape[1] // 4
        span = pl.ds(i * part, part)
        return pltpu.make_async_copy(
            proj_hbm.at[:, span], proj_w.at[:, span], proj_sem.at[i]
        )

    def slab(s):
        return pl.ds(pl.multiple_of(s * width, width), width)

    def gate_copy(t):
        span = slab(ordered(t))
        return pltpu.make_async_copy(
            gate_hbm.at[:, span], gate_w.at[:, span], gate_sem.at[t]
        )

    def up_copy(t):
        span = slab(ordered(t))
        return pltpu.make_async_copy(
            up_hbm.at[:, span], up_w.at[:, span], up_sem.at[t]
        )

    per_row = proj_hbm.shape[1] // hidden_width

    def down_place(t):
        if t < SPARE:
            return down_w.at[t]
        t -= SPARE
        if t < per_row:
            return proj_w.at[:, pl.ds(t * hidden_width, hidden_width)]
        t -= per_row
        return gate_w.at[
            pl.ds(t // per_row * width, width),
            pl.ds(t % per_row * hidden_width, hidden_width),
        ]

    def down_owner(t):
        k, group = t % NZ, t // NZ
        return rank_of(NZ - 1 - k, 1 - group // 2, 1 - group % 2)

    def down_copy(t):
        return pltpu.make_async_copy(
            down_hbm.at[slab(down_owner(t)), :], down_place(t), down_sem.at[t]
        )

    for r in range(rows):
        cache_copy(r).start()
    for i in range(4):
        proj_copy(i).start()

    def start_weights(t, carry):
        gate_copy(t).start()
        up_copy(t).start()
        return carry

    lax.fori_loop(0, n, start_weights, 0)
    for t in range(SPARE):
        down_copy(t).start()

    query_wide = queries_ref[...].astype(jnp.float32)
    for h in range(HQ):
        head_rows[pl.ds(h, rows, stride=HQ), :] = query_wide[:, h * HD : (h + 1) * HD]
    group_size = HQ // KVH
    pair = 2 * group_size
    own_head = lax.broadcasted_iota(jnp.int32, (pair, TILE), 0) // group_size == (
        lax.broadcasted_iota(jnp.int32, (pair, TILE), 1) // HD
    )
    score_scale = 1.0 / math.sqrt(HD)
    for r in range(rows):
        cache_copy(r).wait()

    def attend(*accs):
        pairs = range(KVH // 2)
        for r in range(rows):
            parent = lax.rem(parents_ref[r], rows)
            spreads, news = [], []
            for p in pairs:
                unit, step = p % 2, p // 2
                span = slice(p * TILE, (p + 1) * TILE)
                head_block = head_rows[r * HQ + p * pair : r * HQ + (p + 1) * pair, :]
                spread = jnp.where(own_head, jnp.concatenate([head_block] * 2, axis=1), 0.0)
                push(cache[parent, 0, :, span], step, unit)
                pltpu.matmul_acc_lhs(accs[p], spread.astype(jnp.bfloat16), step)
                new_key = new_kv_ref[r, 0:1, span].astype(jnp.float32)
                news.append(jnp.sum(spread * new_key, axis=1, keepdims=True))
            scores = jnp.concatenate([pltpu.matmul_pop(accs[p]) for p in pairs], axis=0) * score_scale
            score_new = jnp.concatenate(news, axis=0) * score_scale
            top = jnp.maximum(jnp.max(scores, axis=1, keepdims=True), score_new)
            expo = jnp.exp(scores - top)
            expo_new = jnp.exp(score_new - top)
            denom = jnp.sum(expo, axis=1, keepdims=True) + expo_new
            weights = (expo / denom).astype(jnp.bfloat16)
            weight_new = (expo_new / denom).astype(jnp.bfloat16).astype(jnp.float32)
            for p in pairs:
                unit, step = p % 2, p // 2
                span = slice(p * TILE, (p + 1) * TILE)
                own = slice(p * pair, (p + 1) * pair)
                pltpu.matmul_push_rhs(cache[parent, 1, :, span], step, unit)
                pltpu.matmul_acc_lhs(accs[p], weights[own], step)
            for p in pairs:
                span = slice(p * TILE, (p + 1) * TILE)
                new_value = new_kv_ref[r, 1:2, span].astype(jnp.float32)
                mixed = pltpu.matmul_pop(accs[p]) + weight_new[p * pair : (p + 1) * pair] * new_value
                for i in range(2):
                    head_rows[pl.ds(r * HQ + p * pair + i * group_size, group_size), :] = mixed[
                        i * group_size : (i + 1) * group_size, i * HD : (i + 1) * HD
                    ]

    pl.run_scoped(attend, *[pltpu.ACC(p % 2)((pair, TILE), jnp.float32) for p in range(KVH // 2)])
    lines = rows * KVH
    for j in range(group_size):
        own_rows[:, j * HD : (j + 1) * HD] = head_rows[
            pl.ds(j, lines, stride=group_size), :
        ]
    att_slots[me] = own_rows[...].astype(jnp.bfloat16)
    pl.semaphore_wait(barrier, len(peers))

    def gather_ops(slots, send_sem, recv_sem):
        def copy(s, k, device):
            return pltpu.make_async_remote_copy(
                src_ref=slots.at[s],
                dst_ref=slots.at[s],
                send_sem=send_sem.at[k],
                recv_sem=recv_sem.at[s],
                device_id={"blk": device},
                device_id_type=MESH_IDS,
            )

        def begin():
            for q in (3, 2, 1):
                copy(me, q - 1, rank_of(q, 0, 0)).start()
            copy(me, 3, x_peer).start()
            copy(me, 7, core_peer).start()

        def act(arrival):
            q, dx, dc = arrival
            s = rank_of(q, dx, dc)
            copy(s, 0, core_peer).wait_recv()
            if dc == 0 and dx == 0:
                copy(s, 3 + q, x_peer).start()
                copy(s, 7 + q, core_peer).start()
            elif dc == 0:
                copy(s, 11 + q, core_peer).start()

        def finish():
            for k in range(15):
                copy(me, k, core_peer).wait_send()

        return begin, act, finish

    begin, act, finish1 = gather_ops(att_slots, ag1_send, ag1_recv)
    begin()

    for arrival in (own[1], own[3], own[2], over_x[0], over_x[1], over_x[3], over_x[2]):
        act(arrival)
    for arrival in arrivals:
        if arrival[2]:
            act(arrival)

    def widen(s, carry):
        wide = att_slots[s].astype(jnp.float32)
        for j in range(group_size):
            att_wide[j, pl.ds(pl.multiple_of(s * lines, 8), lines), :] = wide[
                :, j * HD : (j + 1) * HD
            ]
        return carry

    lax.fori_loop(0, n, widen, 0)
    for i in range(4):
        proj_copy(i).wait()

    def project(*accs):
        parts = []
        for g in range(KVH):
            for j in range(0, group_size, 2):
                parts.append(
                    jnp.concatenate(
                        [
                            att_wide[j + i, pl.ds(g, total_rows, stride=KVH), :]
                            for i in range(2)
                        ],
                        axis=1,
                    ).astype(jnp.bfloat16)
                )
        return times_transposed(parts, proj_w, accs)

    acc_types = [pltpu.ACC(unit)((total_rows, TILE), jnp.float32) for unit in range(2)]
    projected = pl.run_scoped(project, *acc_types)
    after = (residual_ref[...].astype(jnp.float32) + projected).astype(jnp.bfloat16)
    wide = after.astype(jnp.float32)
    gain = gain_ref[...].astype(jnp.float32).reshape(1, width)
    act_slots[me] = (wide * gain).astype(jnp.bfloat16)
    begin, act, finish2 = gather_ops(act_slots, ag2_send, ag2_recv)
    begin()
    for t in range(SPARE, SPARE + per_row):
        down_copy(t).start()
    after_ref[...] = after

    folded = wide[:, 0:LANES] * wide[:, 0:LANES]
    for j in range(1, width // LANES):
        part = wide[:, j * LANES : (j + 1) * LANES]
        folded = folded + part * part
    squares[0] = folded

    def square_copy(k):
        slot = (0, 2, 4, 4, 4)[k]
        return pltpu.make_async_remote_copy(
            src_ref=squares.at[slot],
            dst_ref=squares.at[(1, 3, 5, 6, 7)[k]],
            send_sem=square_send.at[k],
            recv_sem=square_recv.at[k],
            device_id={"blk": peers[k]},
            device_id_type=MESH_IDS,
        )

    square_copy(0).start()

    def squares_over_cores():
        square_copy(0).wait_recv()
        squares[2] = squares[0] + squares[1]
        square_copy(1).start()

    def squares_over_x():
        square_copy(1).wait_recv()
        squares[4] = squares[2] + squares[3]
        for k in (2, 3, 4):
            square_copy(k).start()

    def feed_forward(*accs):
        gate_accs, up_accs = accs[0::2], accs[1::2]

        def act_all(those):
            for arrival in those:
                act(arrival)

        def consume(t, carry):
            s = ordered(t)
            for i, those in awaited.items():
                pl.when(t == i)(functools.partial(act_all, those))
            pl.when(t == 3)(squares_over_cores)
            pl.when(t == 7)(squares_over_x)
            gate_copy(t).wait()
            up_copy(t).wait()
            for k in range(width // TILE):
                part = act_slots[s, :, k * TILE : (k + 1) * TILE]
                span = pl.ds(pl.multiple_of(s * width + k * TILE, TILE), TILE)
                for i in range(hidden_width // TILE):
                    step = k * (hidden_width // TILE) + i
                    tall = pl.ds(i * TILE, TILE)
                    for unit, weights in enumerate((gate_w, up_w)):
                        push(weights[tall, span], step, unit)
                        pltpu.matmul_acc_lhs((gate_accs, up_accs)[unit][i], part, step % 2)
            return carry

        lax.fori_loop(0, n, consume, 0)
        total = squares[4]
        for k in (2, 3, 4):
            square_copy(k).wait_recv()
            total = total + squares[k + 3]
        inverse_rms = lax.rsqrt(
            jnp.sum(total, axis=1, keepdims=True) / (n * width) + epsilon
        )
        hidden = []
        for gate_acc, up_acc in zip(gate_accs, up_accs):
            gate_sum = pltpu.matmul_pop(gate_acc) * inverse_rms
            up_sum = pltpu.matmul_pop(up_acc) * inverse_rms
            hidden.append((gate_sum / (1.0 + jnp.exp(-gate_sum)) * up_sum).astype(jnp.bfloat16))
        return tuple(hidden)

    hidden = pl.run_scoped(feed_forward, *acc_types * (hidden_width // TILE))
    for t in range(SPARE + per_row, n):
        down_copy(t).start()
    def core_copy(t):
        i = t % NZ + t // (2 * NZ) * NZ
        return pltpu.make_async_remote_copy(
            src_ref=rs_send.at[t],
            dst_ref=core_recv.at[i],
            send_sem=own_send.at[t],
            recv_sem=core_sem.at[i],
            device_id={"blk": core_peer},
            device_id_type=MESH_IDS,
        )

    def x_copy(t):
        return pltpu.make_async_remote_copy(
            src_ref=rs_send.at[t],
            dst_ref=x_recv.at[t % NZ],
            send_sem=own_send.at[t],
            recv_sem=x_sem.at[t % NZ],
            device_id={"blk": x_peer},
            device_id_type=MESH_IDS,
        )

    def z_copy(t):
        return pltpu.make_async_remote_copy(
            src_ref=rs_send.at[t],
            dst_ref=z_recv.at[t % NZ],
            send_sem=own_send.at[t],
            recv_sem=z_sem.at[t % NZ],
            device_id={"blk": rank_of(NZ - 1 - t % NZ, 0, 0)},
            device_id_type=MESH_IDS,
        )

    def term(t):
        down_copy(t).wait()
        return pl.run_scoped(
            lambda *accs: times_transposed(hidden, down_place(t), accs), *acc_types
        )

    sends = []
    for t in (0, 1, 2, 4, 3, 5, 8, 6, 9, 7, 10, 11, 12, 13, 14):
        total = term(t)
        group = t // NZ
        if group % 2 == 1:
            core_copy(t - NZ).wait_recv()
            total = total + core_recv[t % NZ + group // 2 * NZ].astype(jnp.float32)
        if group == 3:
            x_copy(t - 2 * NZ).wait_recv()
            total = total + x_recv[t % NZ].astype(jnp.float32)
        rs_send[t] = total.astype(jnp.bfloat16)
        copy = (core_copy, x_copy, core_copy, z_copy)[group](t)
        copy.start()
        sends.append(copy)
    t = n - 1
    total = term(t)
    core_copy(t - NZ).wait_recv()
    total = total + core_recv[2 * NZ - 1].astype(jnp.float32)
    x_copy(t - 2 * NZ).wait_recv()
    total = total + x_recv[NZ - 1].astype(jnp.float32)
    total = total + after_ref[...].astype(jnp.float32)
    for k in range(NZ - 1):
        z_copy(n - NZ + k).wait_recv()
        total = total + z_recv[k].astype(jnp.float32)
    out_ref[...] = total.astype(jnp.bfloat16)
    for copy in sends:
        copy.wait_send()
    finish1()
    finish2()
    for k in range(len(peers)):
        square_copy(k).wait_send()


def hand_over(after_ref, out_ref, after_to, out_to):
    after_to[...] = after_ref[...]
    out_to[...] = out_ref[...]


def fused_shards(
    queries, new_kv, cache_kv, parents, residual, out_proj, norm_gain, w_gate, w_up, w_down
):
    rows = queries.shape[0]
    n = NZ * NX * NC
    width, depth = out_proj.shape
    hidden_width = w_gate.shape[0]
    total_rows = n * rows
    bf16, f32 = jnp.bfloat16, jnp.float32
    in_vmem = pl.BlockSpec(memory_space=pltpu.VMEM)
    outside = pl.BlockSpec(memory_space=pl.ANY)
    dma = pltpu.SemaphoreType.DMA
    after, out = pl.pallas_call(
        functools.partial(fused_kernel, rows),
        out_shape=(
            jax.ShapeDtypeStruct((total_rows, width), bf16),
            jax.ShapeDtypeStruct((total_rows, width), bf16),
        ),
        in_specs=[pl.BlockSpec(memory_space=pltpu.SMEM)] + [in_vmem] * 4 + [outside] * 5,
        out_specs=(in_vmem, in_vmem),
        scratch_shapes=[
            pltpu.VMEM(cache_kv.shape, bf16),
            pltpu.VMEM((width, depth), bf16),
            pltpu.VMEM((hidden_width, depth), bf16),
            pltpu.VMEM((hidden_width, depth), bf16),
            pltpu.VMEM((SPARE, width, hidden_width), bf16),
            pltpu.VMEM((n, rows * KVH, depth // KVH), bf16),
            pltpu.VMEM((HQ // KVH, total_rows * KVH, HD), f32),
            pltpu.VMEM((rows * HQ, HD), f32),
            pltpu.VMEM((rows * KVH, depth // KVH), f32),
            pltpu.VMEM((n, total_rows, width), bf16),
            pltpu.VMEM((8, total_rows, LANES), f32),
            pltpu.VMEM((n - 1, total_rows, width), bf16),
            pltpu.VMEM((NZ * NX, total_rows, width), bf16),
            pltpu.VMEM((NZ, total_rows, width), bf16),
            pltpu.VMEM((NZ - 1, total_rows, width), bf16),
            dma((rows,)),
            dma((4,)),
            dma((n,)),
            dma((n,)),
            dma((n,)),
            dma((5,)),
            dma((5,)),
            dma((n - 1,)),
            dma((n,)),
            dma((n - 1,)),
            dma((n,)),
            dma((n - 1,)),
            dma((NZ * NX,)),
            dma((NZ,)),
            dma((NZ - 1,)),
        ],
        compiler_params=pltpu.CompilerParams(
            collective_id=0, has_side_effects=True, vmem_limit_bytes=67043328
        ),
        name="layer",
    )(
        parents,
        queries,
        new_kv,
        norm_gain,
        residual.T,
        cache_kv,
        out_proj,
        w_gate,
        w_up,
        w_down,
    )
    after, out = pl.pallas_call(
        hand_over, out_shape=(after, out), in_specs=[in_vmem] * 2, out_specs=(in_vmem, in_vmem)
    )(after, out)
    return after.T, out.T


def solution(mesh):
    fits = mesh.shape["blk"] == NZ * NX * NC
    return jax.shard_map(
        fused_shards if fits else shards,
        mesh=mesh,
        in_specs=(
            P(("groups", "blk"), None),
            P(("groups", "blk"), None, None),
            P(("groups", "blk"), None, None, None),
            P(("groups", "blk")),
            P("blk", "groups"),
            P("blk", None),
            P("blk"),
            P("blk", None),
            P("blk", None),
            P(None, "blk"),
        ),
        out_specs=(P("blk", "groups"), P("blk", "groups")),
        check_vma=False,
    )
```

```python
import functools
import math

import jax
import jax.numpy as jnp
from jax import lax
from jax.experimental import pallas as pl
from jax.experimental.pallas import tpu as pltpu
from jax.sharding import PartitionSpec as P

D = 8192
HQ = 64
KVH = 8
HD = 128
CACHE = 256


epsilon = 1e-06


def attend_rows(queries, new_kv, cache_kv, parents):
    row_count = queries.shape[0]
    group_size = HQ // KVH
    local_parent = parents - lax.axis_index("blk") * row_count
    chosen = jnp.broadcast_to(cache_kv[0], cache_kv.shape)
    for i in range(1, row_count):
        here = (local_parent == i)[:, None, None, None]
        chosen = jnp.where(here, cache_kv[i], chosen)
    cache_keys = chosen[:, 0].reshape(row_count, CACHE, KVH, HD)
    cache_values = chosen[:, 1].reshape(row_count, CACHE, KVH, HD)
    new_key = new_kv[:, 0].reshape(row_count, KVH, HD)
    new_value = new_kv[:, 1].reshape(row_count, KVH, HD)
    query_heads = queries.reshape(row_count, KVH, group_size, HD)
    score_scale = 1.0 / math.sqrt(HD)
    score_cache = (
        jnp.einsum("rgjd,rcgd->rgjc", query_heads, cache_keys, preferred_element_type=jnp.float32)
        * score_scale
    )
    score_new = (
        jnp.einsum("rgjd,rgd->rgj", query_heads, new_key, preferred_element_type=jnp.float32)
        * score_scale
    )
    score_top = jnp.maximum(jnp.max(score_cache, axis=-1), score_new)
    expo_cache = jnp.exp(score_cache - score_top[..., None])
    expo_new = jnp.exp(score_new - score_top)
    denom_sum = jnp.sum(expo_cache, axis=-1) + expo_new
    weight_cache = (expo_cache / denom_sum[..., None]).astype(jnp.bfloat16)
    weight_new = (expo_new / denom_sum).astype(jnp.bfloat16)
    mixed_heads = jnp.einsum(
        "rgjc,rcgd->rgjd", weight_cache, cache_values, preferred_element_type=jnp.float32
    )
    mixed_heads = (
        mixed_heads
        + weight_new.astype(jnp.float32)[..., None] * new_value.astype(jnp.float32)[:, :, None, :]
    )
    return mixed_heads.reshape(row_count, HQ * HD).astype(jnp.bfloat16)


def shards(queries, new_kv, cache_kv, parents, residual, out_proj, norm_gain, w_gate, w_up, w_down):
    attended = attend_rows(queries, new_kv, cache_kv, parents)
    projected = lax.dot_general(
        out_proj,
        lax.all_gather(attended, "blk", axis=0, tiled=True),
        (((1,), (1,)), ((), ())),
        preferred_element_type=jnp.float32,
    )
    after_attention = (residual.astype(jnp.float32) + projected).astype(jnp.bfloat16)
    widened = after_attention.astype(jnp.float32)
    gathered, gain_all = (
        lax.all_gather(after_attention, "blk", axis=0, tiled=True),
        lax.all_gather(norm_gain, "blk", axis=0, tiled=True),
    )
    gathered_wide = gathered.astype(jnp.float32)
    inverse_rms = lax.rsqrt(jnp.sum(gathered_wide * gathered_wide, axis=0) / D + epsilon)
    normed_all = (
        gathered_wide * inverse_rms[None, :] * gain_all.astype(jnp.float32)[:, None]
    ).astype(jnp.bfloat16)
    gate_sum = jnp.dot(w_gate, normed_all, preferred_element_type=jnp.float32)
    up_sum = jnp.dot(w_up, normed_all, preferred_element_type=jnp.float32)
    hidden = (jax.nn.silu(gate_sum) * up_sum).astype(jnp.bfloat16)
    ffn_delta = lax.psum_scatter(
        jnp.dot(w_down, hidden, preferred_element_type=jnp.float32),
        "blk",
        scatter_dimension=0,
        tiled=True,
    )
    layer_out = (widened + ffn_delta).astype(jnp.bfloat16)
    return (after_attention, layer_out)


LANES = 128
TILE = 256
NZ, NX, NC = 4, 2, 2
SPARE = 3
MESH_IDS = pl.DeviceIdType.MESH
NT = (((1,), (1,)), ((), ()))


def push(tile, step, unit):
    if (step + unit) % 5 in (0, 2):
        pltpu.matmul_push_rhs(tile, step % 2, unit, transpose=True)
    else:
        pltpu.matmul_push_rhs(tile.T, step % 2, unit)


def times_transposed(parts, weights, accs):
    for k, part in enumerate(parts):
        for unit, acc in enumerate(accs):
            push(weights[unit * TILE : (unit + 1) * TILE, k * TILE : (k + 1) * TILE], k, unit)
            pltpu.matmul_acc_lhs(acc, part, k % 2)
    return jnp.concatenate([pltpu.matmul_pop(acc) for acc in accs], axis=1)


def fused_kernel(
    rows,
    parents_ref,
    queries_ref,
    new_kv_ref,
    gain_ref,
    residual_ref,
    cache_hbm,
    proj_hbm,
    gate_hbm,
    up_hbm,
    down_hbm,
    after_ref,
    out_ref,
    keys,
    values,
    proj_w,
    gate_w,
    up_w,
    down_w,
    att_slots,
    att_wide,
    head_rows,
    own_rows,
    act_slots,
    squares,
    rs_send,
    core_recv,
    x_recv,
    z_recv,
    cache_sem,
    proj_sem,
    gate_sem,
    up_sem,
    down_sem,
    square_send,
    square_recv,
    ag1_send,
    ag1_recv,
    ag2_send,
    ag2_recv,
    own_send,
    core_sem,
    x_sem,
    z_sem,
):
    me = lax.axis_index("blk")
    core = lax.rem(me, NC)
    along_x = lax.rem(lax.div(me, NC), NX)
    along_z = lax.div(me, NC * NX)
    n = NZ * NX * NC
    width = proj_hbm.shape[0]
    hidden_width = gate_hbm.shape[0]
    total_rows = n * rows

    z_places = (
        along_z,
        along_z + 1 - 2 * lax.rem(along_z, 2),
        NZ - 1 - along_z,
        lax.rem(along_z + 2, NZ),
    )

    def pick(values, t):
        chosen = jnp.int32(values[-1])
        for i in range(len(values) - 1):
            chosen = jnp.where(t == i, values[i], chosen)
        return chosen

    def rank_of(q, dx, dc):
        return (
            z_places[q] * (NX * NC)
            + lax.rem(along_x + dx, NX) * NC
            + lax.rem(core + dc, NC)
        )

    x_peer = rank_of(0, 1, 0)
    core_peer = rank_of(0, 0, 1)

    arrivals = [(0, 0, 0), (0, 0, 1), (1, 0, 0), (0, 1, 0), (1, 0, 1), (0, 1, 1)]
    arrivals += [(2, 0, 0), (3, 0, 0), (2, 0, 1), (3, 0, 1), (1, 1, 0), (1, 1, 1)]
    arrivals += [(2, 1, 0), (3, 1, 0), (2, 1, 1), (3, 1, 1)]
    awaited = {1: "c0", 2: "z1", 3: "x0", 4: "c1", 5: "cx0", 6: "z2 z3", 8: "x1 c2", 11: "cx1", 12: "x2", 14: "cx2"}

    def ordered(t):
        return pick([rank_of(*arrival) for arrival in arrivals], t)

    barrier = pltpu.get_barrier_semaphore()
    z_peers = [rank_of(q, 0, 0) for q in range(1, NZ)]
    peers = [core_peer, x_peer] + z_peers
    for peer in peers:
        pl.semaphore_signal(
            barrier, inc=1, device_id={"blk": peer}, device_id_type=MESH_IDS
        )

    def cache_copy(r, i):
        return pltpu.make_async_copy(
            cache_hbm.at[r, i], (keys, values)[i].at[r], cache_sem.at[r, i]
        )

    def proj_copy(i):
        part = proj_hbm.shape[1] // 4
        span = pl.ds(i * part, part)
        return pltpu.make_async_copy(
            proj_hbm.at[:, span], proj_w.at[:, span], proj_sem.at[i]
        )

    def slab(s):
        return pl.ds(pl.multiple_of(s * width, width), width)

    def gate_copy(t):
        span = slab(ordered(t))
        return pltpu.make_async_copy(
            gate_hbm.at[:, span], gate_w.at[:, span], gate_sem.at[t]
        )

    def up_copy(t):
        span = slab(ordered(t))
        return pltpu.make_async_copy(
            up_hbm.at[:, span], up_w.at[:, span], up_sem.at[t]
        )

    per_row = proj_hbm.shape[1] // hidden_width

    def down_place(t):
        if t < SPARE:
            return down_w.at[t]
        t -= SPARE
        if t < per_row:
            return proj_w.at[:, pl.ds(t * hidden_width, hidden_width)]
        t -= per_row
        return gate_w.at[
            pl.ds(t // per_row * width, width),
            pl.ds(t % per_row * hidden_width, hidden_width),
        ]

    def down_owner(t):
        k, group = t % NZ, t // NZ
        return rank_of(NZ - 1 - k, 1 - group // 2, 1 - group % 2)

    def down_copy(t):
        return pltpu.make_async_copy(
            down_hbm.at[slab(down_owner(t)), :], down_place(t), down_sem.at[t]
        )

    for i in range(2):
        for r in range(rows):
            cache_copy(r, i).start()
    for i in range(4):
        proj_copy(i).start()

    def start_weights(t, carry):
        gate_copy(t).start()
        up_copy(t).start()
        return carry

    lax.fori_loop(0, n, start_weights, 0)
    for t in range(SPARE):
        down_copy(t).start()

    query_wide = queries_ref[...].astype(jnp.float32)
    for h in range(HQ):
        head_rows[pl.ds(h, rows, stride=HQ), :] = query_wide[:, h * HD : (h + 1) * HD]
    group_size = HQ // KVH
    pair = 2 * group_size
    own_head = lax.broadcasted_iota(jnp.int32, (pair, TILE), 0) // group_size == (
        lax.broadcasted_iota(jnp.int32, (pair, TILE), 1) // HD
    )
    score_scale = 1.0 / math.sqrt(HD)
    for r in range(rows):
        cache_copy(r, 0).wait()

    pairs = range(KVH // 2)

    def columns(p):
        return slice(p * TILE, (p + 1) * TILE)

    def attend(*accs):
        parents = [lax.rem(parents_ref[r], rows) for r in range(rows)]
        news, weights, weights_new = [], [], []
        for r in range(rows):
            for p in pairs:
                head_block = head_rows[r * HQ + p * pair : r * HQ + (p + 1) * pair, :]
                spread = jnp.where(own_head, jnp.concatenate([head_block] * 2, axis=1), 0.0)
                step = 2 * r + p // 2
                push(keys[parents[r], :, columns(p)], step, p % 2)
                pltpu.matmul_acc_lhs(accs[r * len(pairs) + p], spread.astype(jnp.bfloat16), step % 2)
                new_key = new_kv_ref[r, 0:1, columns(p)].astype(jnp.float32)
                news.append(jnp.sum(spread * new_key, axis=1, keepdims=True))
        for r in range(rows):
            own_accs = accs[r * len(pairs) : (r + 1) * len(pairs)]
            scores = jnp.concatenate([pltpu.matmul_pop(acc) for acc in own_accs], axis=0) * score_scale
            score_new = (
                jnp.concatenate(news[r * len(pairs) : (r + 1) * len(pairs)], axis=0) * score_scale
            )
            top = jnp.maximum(jnp.max(scores, axis=1, keepdims=True), score_new)
            expo = jnp.exp(scores - top)
            expo_new = jnp.exp(score_new - top)
            denom = jnp.sum(expo, axis=1, keepdims=True) + expo_new
            weights.append((expo / denom).astype(jnp.bfloat16))
            weights_new.append((expo_new / denom).astype(jnp.bfloat16).astype(jnp.float32))
        for r in range(rows):
            cache_copy(r, 1).wait()
        for r in range(rows):
            for p in pairs:
                step = 2 * r + p // 2
                pltpu.matmul_push_rhs(values[parents[r], :, columns(p)], step % 2, p % 2)
                pltpu.matmul_acc_lhs(
                    accs[r * len(pairs) + p], weights[r][p * pair : (p + 1) * pair], step % 2
                )
        for r in range(rows):
            for p in pairs:
                new_value = new_kv_ref[r, 1:2, columns(p)].astype(jnp.float32)
                mixed = pltpu.matmul_pop(accs[r * len(pairs) + p])
                mixed = mixed + weights_new[r][p * pair : (p + 1) * pair] * new_value
                for i in range(2):
                    head_rows[pl.ds(r * HQ + p * pair + i * group_size, group_size), :] = mixed[
                        i * group_size : (i + 1) * group_size, i * HD : (i + 1) * HD
                    ]

    pl.run_scoped(
        attend, *[pltpu.ACC(p % 2)((pair, TILE), jnp.float32) for r in range(rows) for p in pairs]
    )
    lines = rows * KVH
    for j in range(group_size):
        own_rows[:, j * HD : (j + 1) * HD] = head_rows[
            pl.ds(j, lines, stride=group_size), :
        ]
    att_slots[0] = own_rows[...].astype(jnp.bfloat16)
    pl.semaphore_wait(barrier, len(peers))

    def gather_ops(slots, send_sem, recv_sem):
        def copy(first, to, count, k, device):
            return pltpu.make_async_remote_copy(
                src_ref=slots.at[pl.ds(first, count)],
                dst_ref=slots.at[pl.ds(to, count)],
                send_sem=send_sem.at[k],
                recv_sem=recv_sem.at[k],
                device_id={"blk": device},
                device_id_type=MESH_IDS,
            )

        x, c, xc = 2 * NZ, NZ, 3 * NZ
        copies = {
            "z1": copy(0, 1, 1, 0, rank_of(1, 0, 0)),
            "z2": copy(0, 2, 1, 1, rank_of(2, 0, 0)),
            "z3": copy(0, 3, 1, 2, rank_of(3, 0, 0)),
            "x0": copy(0, x, 1, 3, x_peer),
            "x1": copy(1, x + 1, 1, 4, x_peer),
            "x2": copy(2, x + 2, 2, 5, x_peer),
            "c0": copy(0, c, 1, 6, core_peer),
            "c1": copy(1, c + 1, 1, 7, core_peer),
            "c2": copy(2, c + 2, 2, 8, core_peer),
            "cx0": copy(x, xc, 1, 9, core_peer),
            "cx1": copy(x + 1, xc + 1, 1, 10, core_peer),
            "cx2": copy(x + 2, xc + 2, 2, 11, core_peer),
        }
        then = {"z1": "x1 c1", "z3": "x2 c2", "x0": "cx0", "x1": "cx1", "x2": "cx2"}

        def begin():
            for name in ("z3", "z2", "z1", "x0", "c0"):
                copies[name].start()

        def act(names):
            for name in names.split():
                copies[name].wait_recv()
                for following in then.get(name, "").split():
                    copies[following].start()

        def finish():
            for each in copies.values():
                each.wait_send()

        return begin, act, finish

    begin, act, finish1 = gather_ops(att_slots, ag1_send, ag1_recv)
    begin()

    for names in ("z1 z2 z3", "x0 x1 x2", "c0 c1 c2", "cx0 cx1 cx2"):
        act(names)
    for q, dx, dc in arrivals:
        wide = att_slots[NZ * (2 * dx + dc) + q].astype(jnp.float32)
        at = pl.ds(pl.multiple_of(rank_of(q, dx, dc) * lines, 8), lines)
        for j in range(group_size):
            att_wide[j, at, :] = wide[:, j * HD : (j + 1) * HD]
    for i in range(4):
        proj_copy(i).wait()

    def project(*accs):
        parts = []
        for g in range(KVH):
            for j in range(0, group_size, 2):
                parts.append(
                    jnp.concatenate(
                        [
                            att_wide[j + i, pl.ds(g, total_rows, stride=KVH), :]
                            for i in range(2)
                        ],
                        axis=1,
                    ).astype(jnp.bfloat16)
                )
        return times_transposed(parts, proj_w, accs)

    acc_types = [pltpu.ACC(unit)((total_rows, TILE), jnp.float32) for unit in range(2)]
    projected = pl.run_scoped(project, *acc_types)
    after = (residual_ref[...].astype(jnp.float32) + projected).astype(jnp.bfloat16)
    wide = after.astype(jnp.float32)
    gain = gain_ref[...].astype(jnp.float32).reshape(1, width)
    act_slots[0] = (wide * gain).astype(jnp.bfloat16)
    begin, act, finish2 = gather_ops(act_slots, ag2_send, ag2_recv)
    begin()
    for t in range(SPARE, SPARE + per_row):
        down_copy(t).start()
    after_ref[...] = after

    folded = wide[:, 0:LANES] * wide[:, 0:LANES]
    for j in range(1, width // LANES):
        part = wide[:, j * LANES : (j + 1) * LANES]
        folded = folded + part * part
    squares[0] = folded

    def square_copy(k):
        slot = (0, 2, 4, 4, 4)[k]
        return pltpu.make_async_remote_copy(
            src_ref=squares.at[slot],
            dst_ref=squares.at[(1, 3, 5, 6, 7)[k]],
            send_sem=square_send.at[k],
            recv_sem=square_recv.at[k],
            device_id={"blk": peers[k]},
            device_id_type=MESH_IDS,
        )

    square_copy(0).start()

    def squares_over_cores():
        square_copy(0).wait_recv()
        squares[2] = squares[0] + squares[1]
        square_copy(1).start()

    def squares_over_x():
        square_copy(1).wait_recv()
        squares[4] = squares[2] + squares[3]
        for k in (2, 3, 4):
            square_copy(k).start()

    def feed_forward(*accs):
        gate_accs, up_accs = accs[0::2], accs[1::2]

        for t, (q, dx, dc) in enumerate(arrivals):
            s = rank_of(q, dx, dc)
            act(awaited.get(t, ""))
            if t == 3:
                squares_over_cores()
            if t == 7:
                squares_over_x()
            gate_copy(t).wait()
            up_copy(t).wait()
            for k in range(width // TILE):
                part = act_slots[NZ * (2 * dx + dc) + q, :, k * TILE : (k + 1) * TILE]
                span = pl.ds(pl.multiple_of(s * width + k * TILE, TILE), TILE)
                for i in range(hidden_width // TILE):
                    step = k * (hidden_width // TILE) + i
                    tall = pl.ds(i * TILE, TILE)
                    for unit, weights in enumerate((gate_w, up_w)):
                        push(weights[tall, span], step, unit)
                        pltpu.matmul_acc_lhs((gate_accs, up_accs)[unit][i], part, step % 2)
        total = squares[4]
        for k in (2, 3, 4):
            square_copy(k).wait_recv()
            total = total + squares[k + 3]
        inverse_rms = lax.rsqrt(
            jnp.sum(total, axis=1, keepdims=True) / (n * width) + epsilon
        )
        hidden = []
        for gate_acc, up_acc in zip(gate_accs, up_accs):
            gate_sum = pltpu.matmul_pop(gate_acc) * inverse_rms
            up_sum = pltpu.matmul_pop(up_acc) * inverse_rms
            hidden.append((gate_sum / (1.0 + jnp.exp(-gate_sum)) * up_sum).astype(jnp.bfloat16))
        return tuple(hidden)

    hidden = pl.run_scoped(feed_forward, *acc_types * (hidden_width // TILE))
    for t in range(SPARE + per_row, n):
        down_copy(t).start()
    def core_copy(t):
        i = t % NZ + t // (2 * NZ) * NZ
        return pltpu.make_async_remote_copy(
            src_ref=rs_send.at[t],
            dst_ref=core_recv.at[i],
            send_sem=own_send.at[t],
            recv_sem=core_sem.at[i],
            device_id={"blk": core_peer},
            device_id_type=MESH_IDS,
        )

    def x_copy(t):
        return pltpu.make_async_remote_copy(
            src_ref=rs_send.at[t],
            dst_ref=x_recv.at[t % NZ],
            send_sem=own_send.at[t],
            recv_sem=x_sem.at[t % NZ],
            device_id={"blk": x_peer},
            device_id_type=MESH_IDS,
        )

    def z_copy(t):
        return pltpu.make_async_remote_copy(
            src_ref=rs_send.at[t],
            dst_ref=z_recv.at[t % NZ],
            send_sem=own_send.at[t],
            recv_sem=z_sem.at[t % NZ],
            device_id={"blk": rank_of(NZ - 1 - t % NZ, 0, 0)},
            device_id_type=MESH_IDS,
        )

    def term(t):
        down_copy(t).wait()
        return pl.run_scoped(
            lambda *accs: times_transposed(hidden, down_place(t), accs), *acc_types
        )

    sends = []
    for t in (0, 1, 2, 4, 3, 5, 8, 6, 9, 7, 10, 11, 12, 13, 14):
        total = term(t)
        group = t // NZ
        if group % 2 == 1:
            core_copy(t - NZ).wait_recv()
            total = total + core_recv[t % NZ + group // 2 * NZ].astype(jnp.float32)
        if group == 3:
            x_copy(t - 2 * NZ).wait_recv()
            total = total + x_recv[t % NZ].astype(jnp.float32)
        rs_send[t] = total.astype(jnp.bfloat16)
        copy = (core_copy, x_copy, core_copy, z_copy)[group](t)
        copy.start()
        sends.append(copy)
    t = n - 1
    total = term(t)
    core_copy(t - NZ).wait_recv()
    total = total + core_recv[2 * NZ - 1].astype(jnp.float32)
    x_copy(t - 2 * NZ).wait_recv()
    total = total + x_recv[NZ - 1].astype(jnp.float32)
    total = total + after_ref[...].astype(jnp.float32)
    for k in range(NZ - 1):
        z_copy(n - NZ + k).wait_recv()
        total = total + z_recv[k].astype(jnp.float32)
    out_ref[...] = total.astype(jnp.bfloat16)
    for copy in sends:
        copy.wait_send()
    finish1()
    finish2()
    for k in range(len(peers)):
        square_copy(k).wait_send()


def hand_over(after_ref, out_ref, after_to, out_to):
    after_to[...] = after_ref[...]
    out_to[...] = out_ref[...]


def fused_shards(
    queries, new_kv, cache_kv, parents, residual, out_proj, norm_gain, w_gate, w_up, w_down
):
    rows = queries.shape[0]
    n = NZ * NX * NC
    width, depth = out_proj.shape
    hidden_width = w_gate.shape[0]
    total_rows = n * rows
    bf16, f32 = jnp.bfloat16, jnp.float32
    in_vmem = pl.BlockSpec(memory_space=pltpu.VMEM)
    outside = pl.BlockSpec(memory_space=pl.ANY)
    dma = pltpu.SemaphoreType.DMA
    after, out = pl.pallas_call(
        functools.partial(fused_kernel, rows),
        out_shape=(
            jax.ShapeDtypeStruct((total_rows, width), bf16),
            jax.ShapeDtypeStruct((total_rows, width), bf16),
        ),
        in_specs=[pl.BlockSpec(memory_space=pltpu.SMEM)] + [in_vmem] * 4 + [outside] * 5,
        out_specs=(in_vmem, in_vmem),
        scratch_shapes=[
            pltpu.VMEM((rows, CACHE, KVH * HD), bf16),
            pltpu.VMEM((rows, CACHE, KVH * HD), bf16),
            pltpu.VMEM((width, depth), bf16),
            pltpu.VMEM((hidden_width, depth), bf16),
            pltpu.VMEM((hidden_width, depth), bf16),
            pltpu.VMEM((SPARE, width, hidden_width), bf16),
            pltpu.VMEM((n, rows * KVH, depth // KVH), bf16),
            pltpu.VMEM((HQ // KVH, total_rows * KVH, HD), f32),
            pltpu.VMEM((rows * HQ, HD), f32),
            pltpu.VMEM((rows * KVH, depth // KVH), f32),
            pltpu.VMEM((n, total_rows, width), bf16),
            pltpu.VMEM((8, total_rows, LANES), f32),
            pltpu.VMEM((n - 1, total_rows, width), bf16),
            pltpu.VMEM((NZ * NX, total_rows, width), bf16),
            pltpu.VMEM((NZ, total_rows, width), bf16),
            pltpu.VMEM((NZ - 1, total_rows, width), bf16),
            dma((rows, 2)),
            dma((4,)),
            dma((n,)),
            dma((n,)),
            dma((n,)),
            dma((5,)),
            dma((5,)),
            dma((12,)),
            dma((12,)),
            dma((12,)),
            dma((12,)),
            dma((n - 1,)),
            dma((NZ * NX,)),
            dma((NZ,)),
            dma((NZ - 1,)),
        ],
        compiler_params=pltpu.CompilerParams(
            collective_id=0, has_side_effects=True, vmem_limit_bytes=67043328
        ),
        name="layer",
    )(
        parents,
        queries,
        new_kv,
        norm_gain,
        residual.T,
        cache_kv,
        out_proj,
        w_gate,
        w_up,
        w_down,
    )
    after, out = pl.pallas_call(
        hand_over, out_shape=(after, out), in_specs=[in_vmem] * 2, out_specs=(in_vmem, in_vmem)
    )(after, out)
    return after.T, out.T


def solution(mesh):
    fits = mesh.shape["blk"] == NZ * NX * NC
    return jax.shard_map(
        fused_shards if fits else shards,
        mesh=mesh,
        in_specs=(
            P(("groups", "blk"), None),
            P(("groups", "blk"), None, None),
            P(("groups", "blk"), None, None, None),
            P(("groups", "blk")),
            P("blk", "groups"),
            P("blk", None),
            P("blk"),
            P("blk", None),
            P("blk", None),
            P(None, "blk"),
        ),
        out_specs=(P("blk", "groups"), P("blk", "groups")),
        check_vma=False,
    )
```

```python
import functools
import math

import jax
import jax.numpy as jnp
from jax import lax
from jax.experimental import pallas as pl
from jax.experimental.pallas import tpu as pltpu
from jax.sharding import PartitionSpec as P

D = 8192
HQ = 64
KVH = 8
HD = 128
CACHE = 256


epsilon = 1e-06


def attend_rows(queries, new_kv, cache_kv, parents):
    row_count = queries.shape[0]
    group_size = HQ // KVH
    local_parent = parents - lax.axis_index("blk") * row_count
    chosen = jnp.broadcast_to(cache_kv[0], cache_kv.shape)
    for i in range(1, row_count):
        here = (local_parent == i)[:, None, None, None]
        chosen = jnp.where(here, cache_kv[i], chosen)
    cache_keys = chosen[:, 0].reshape(row_count, CACHE, KVH, HD)
    cache_values = chosen[:, 1].reshape(row_count, CACHE, KVH, HD)
    new_key = new_kv[:, 0].reshape(row_count, KVH, HD)
    new_value = new_kv[:, 1].reshape(row_count, KVH, HD)
    query_heads = queries.reshape(row_count, KVH, group_size, HD)
    score_scale = 1.0 / math.sqrt(HD)
    score_cache = (
        jnp.einsum("rgjd,rcgd->rgjc", query_heads, cache_keys, preferred_element_type=jnp.float32)
        * score_scale
    )
    score_new = (
        jnp.einsum("rgjd,rgd->rgj", query_heads, new_key, preferred_element_type=jnp.float32)
        * score_scale
    )
    score_top = jnp.maximum(jnp.max(score_cache, axis=-1), score_new)
    expo_cache = jnp.exp(score_cache - score_top[..., None])
    expo_new = jnp.exp(score_new - score_top)
    denom_sum = jnp.sum(expo_cache, axis=-1) + expo_new
    weight_cache = (expo_cache / denom_sum[..., None]).astype(jnp.bfloat16)
    weight_new = (expo_new / denom_sum).astype(jnp.bfloat16)
    mixed_heads = jnp.einsum(
        "rgjc,rcgd->rgjd", weight_cache, cache_values, preferred_element_type=jnp.float32
    )
    mixed_heads = (
        mixed_heads
        + weight_new.astype(jnp.float32)[..., None] * new_value.astype(jnp.float32)[:, :, None, :]
    )
    return mixed_heads.reshape(row_count, HQ * HD).astype(jnp.bfloat16)


def shards(queries, new_kv, cache_kv, parents, residual, out_proj, norm_gain, w_gate, w_up, w_down):
    attended = attend_rows(queries, new_kv, cache_kv, parents)
    projected = lax.dot_general(
        out_proj,
        lax.all_gather(attended, "blk", axis=0, tiled=True),
        (((1,), (1,)), ((), ())),
        preferred_element_type=jnp.float32,
    )
    after_attention = (residual.astype(jnp.float32) + projected).astype(jnp.bfloat16)
    widened = after_attention.astype(jnp.float32)
    gathered, gain_all = (
        lax.all_gather(after_attention, "blk", axis=0, tiled=True),
        lax.all_gather(norm_gain, "blk", axis=0, tiled=True),
    )
    gathered_wide = gathered.astype(jnp.float32)
    inverse_rms = lax.rsqrt(jnp.sum(gathered_wide * gathered_wide, axis=0) / D + epsilon)
    normed_all = (
        gathered_wide * inverse_rms[None, :] * gain_all.astype(jnp.float32)[:, None]
    ).astype(jnp.bfloat16)
    gate_sum = jnp.dot(w_gate, normed_all, preferred_element_type=jnp.float32)
    up_sum = jnp.dot(w_up, normed_all, preferred_element_type=jnp.float32)
    hidden = (jax.nn.silu(gate_sum) * up_sum).astype(jnp.bfloat16)
    ffn_delta = lax.psum_scatter(
        jnp.dot(w_down, hidden, preferred_element_type=jnp.float32),
        "blk",
        scatter_dimension=0,
        tiled=True,
    )
    layer_out = (widened + ffn_delta).astype(jnp.bfloat16)
    return (after_attention, layer_out)


LANES = 128
TILE = 256
NZ, NX, NC = 4, 2, 2
SPARE = 3
MESH_IDS = pl.DeviceIdType.MESH
NT = (((1,), (1,)), ((), ()))


def push(tile, step, unit):
    if (step + unit) % 5 in (0, 2):
        pltpu.matmul_push_rhs(tile, step % 2, unit, transpose=True)
    else:
        pltpu.matmul_push_rhs(tile.T, step % 2, unit)


def times_transposed(parts, weights, accs):
    for k, part in enumerate(parts):
        for unit, acc in enumerate(accs):
            push(weights[unit * TILE : (unit + 1) * TILE, k * TILE : (k + 1) * TILE], k, unit)
            pltpu.matmul_acc_lhs(acc, part, k % 2)
    return jnp.concatenate([pltpu.matmul_pop(acc) for acc in accs], axis=1)


def fused_kernel(
    rows,
    parents_ref,
    queries_ref,
    new_kv_ref,
    gain_ref,
    residual_ref,
    cache_hbm,
    proj_hbm,
    gate_hbm,
    up_hbm,
    down_hbm,
    after_ref,
    out_ref,
    keys,
    values,
    proj_w,
    gate_w,
    up_w,
    down_w,
    att_slots,
    att_wide,
    head_rows,
    own_rows,
    act_slots,
    squares,
    rs_send,
    core_recv,
    x_recv,
    z_recv,
    cache_sem,
    proj_sem,
    gate_sem,
    up_sem,
    down_sem,
    square_send,
    square_recv,
    ag1_send,
    ag1_recv,
    ag2_send,
    ag2_recv,
    own_send,
    core_sem,
    x_sem,
    z_sem,
):
    me = lax.axis_index("blk")
    core = lax.rem(me, NC)
    along_x = lax.rem(lax.div(me, NC), NX)
    along_z = lax.div(me, NC * NX)
    n = NZ * NX * NC
    width = proj_hbm.shape[0]
    hidden_width = gate_hbm.shape[0]
    total_rows = n * rows

    z_places = (
        along_z,
        along_z + 1 - 2 * lax.rem(along_z, 2),
        NZ - 1 - along_z,
        lax.rem(along_z + 2, NZ),
    )

    def pick(values, t):
        chosen = jnp.int32(values[-1])
        for i in range(len(values) - 1):
            chosen = jnp.where(t == i, values[i], chosen)
        return chosen

    def rank_of(q, dx, dc):
        return (
            z_places[q] * (NX * NC)
            + lax.rem(along_x + dx, NX) * NC
            + lax.rem(core + dc, NC)
        )

    x_peer = rank_of(0, 1, 0)
    core_peer = rank_of(0, 0, 1)

    arrivals = [(0, 0, 0), (0, 0, 1), (1, 0, 0), (0, 1, 0), (1, 0, 1), (0, 1, 1)]
    arrivals += [(2, 0, 0), (3, 0, 0), (2, 0, 1), (3, 0, 1), (1, 1, 0), (1, 1, 1)]
    arrivals += [(2, 1, 0), (3, 1, 0), (2, 1, 1), (3, 1, 1)]
    awaited = {1: "c0", 2: "z1", 3: "x0", 4: "c1", 5: "cx0", 6: "z2 z3", 8: "x1 c2", 11: "cx1", 12: "x2", 14: "cx2"}

    def ordered(t):
        return pick([rank_of(*arrival) for arrival in arrivals], t)

    barrier = pltpu.get_barrier_semaphore()
    z_peers = [rank_of(q, 0, 0) for q in range(1, NZ)]
    peers = [core_peer, x_peer] + z_peers
    for peer in peers:
        pl.semaphore_signal(
            barrier, inc=1, device_id={"blk": peer}, device_id_type=MESH_IDS
        )

    def cache_copy(r, i):
        return pltpu.make_async_copy(
            cache_hbm.at[r, i], (keys, values)[i].at[r], cache_sem.at[r, i]
        )

    def proj_copy(i):
        part = proj_hbm.shape[1] // 4
        span = pl.ds(i * part, part)
        return pltpu.make_async_copy(
            proj_hbm.at[:, span], proj_w.at[:, span], proj_sem.at[i]
        )

    def slab(s):
        return pl.ds(pl.multiple_of(s * width, width), width)

    def gate_copy(t):
        span = slab(ordered(t))
        return pltpu.make_async_copy(
            gate_hbm.at[:, span], gate_w.at[:, span], gate_sem.at[t]
        )

    def up_copy(t):
        span = slab(ordered(t))
        return pltpu.make_async_copy(
            up_hbm.at[:, span], up_w.at[:, span], up_sem.at[t]
        )

    per_row = proj_hbm.shape[1] // hidden_width

    def down_place(t):
        if t < SPARE:
            return down_w.at[t]
        t -= SPARE
        if t < per_row:
            return proj_w.at[:, pl.ds(t * hidden_width, hidden_width)]
        t -= per_row
        return gate_w.at[
            pl.ds(t // per_row * width, width),
            pl.ds(t % per_row * hidden_width, hidden_width),
        ]

    def down_owner(t):
        k, group = t % NZ, t // NZ
        return rank_of(NZ - 1 - k, 1 - group // 2, 1 - group % 2)

    def down_copy(t):
        return pltpu.make_async_copy(
            down_hbm.at[slab(down_owner(t)), :], down_place(t), down_sem.at[t]
        )

    for i in range(2):
        for r in range(rows):
            cache_copy(r, i).start()
    for i in range(4):
        proj_copy(i).start()

    def start_weights(t, carry):
        gate_copy(t).start()
        up_copy(t).start()
        return carry

    lax.fori_loop(0, n, start_weights, 0)
    for t in range(SPARE):
        down_copy(t).start()

    query_wide = queries_ref[...].astype(jnp.float32)
    for h in range(HQ):
        head_rows[pl.ds(h, rows, stride=HQ), :] = query_wide[:, h * HD : (h + 1) * HD]
    group_size = HQ // KVH
    pair = 2 * group_size
    own_head = lax.broadcasted_iota(jnp.int32, (pair, TILE), 0) // group_size == (
        lax.broadcasted_iota(jnp.int32, (pair, TILE), 1) // HD
    )
    score_scale = 1.0 / math.sqrt(HD)
    for r in range(rows):
        cache_copy(r, 0).wait()

    pairs = range(KVH // 2)

    def columns(p):
        return slice(p * TILE, (p + 1) * TILE)

    def attend(*accs):
        parents = [lax.rem(parents_ref[r], rows) for r in range(rows)]
        news, weights, weights_new = [], [], []
        for r in range(rows):
            for p in pairs:
                head_block = head_rows[r * HQ + p * pair : r * HQ + (p + 1) * pair, :]
                spread = jnp.where(own_head, jnp.concatenate([head_block] * 2, axis=1), 0.0)
                step = 2 * r + p // 2
                push(keys[parents[r], :, columns(p)], step, p % 2)
                pltpu.matmul_acc_lhs(accs[r * len(pairs) + p], spread.astype(jnp.bfloat16), step % 2)
                new_key = new_kv_ref[r, 0:1, columns(p)].astype(jnp.float32)
                news.append(jnp.sum(spread * new_key, axis=1, keepdims=True))
        for r in range(rows):
            own_accs = accs[r * len(pairs) : (r + 1) * len(pairs)]
            scores = jnp.concatenate([pltpu.matmul_pop(acc) for acc in own_accs], axis=0) * score_scale
            score_new = (
                jnp.concatenate(news[r * len(pairs) : (r + 1) * len(pairs)], axis=0) * score_scale
            )
            top = jnp.maximum(jnp.max(scores, axis=1, keepdims=True), score_new)
            expo = jnp.exp(scores - top)
            expo_new = jnp.exp(score_new - top)
            denom = jnp.sum(expo, axis=1, keepdims=True) + expo_new
            weights.append((expo / denom).astype(jnp.bfloat16))
            weights_new.append((expo_new / denom).astype(jnp.bfloat16).astype(jnp.float32))
        for r in range(rows):
            cache_copy(r, 1).wait()
        for r in range(rows):
            for p in pairs:
                step = 2 * r + p // 2
                pltpu.matmul_push_rhs(values[parents[r], :, columns(p)], step % 2, p % 2)
                pltpu.matmul_acc_lhs(
                    accs[r * len(pairs) + p], weights[r][p * pair : (p + 1) * pair], step % 2
                )
        for r in range(rows):
            for p in pairs:
                new_value = new_kv_ref[r, 1:2, columns(p)].astype(jnp.float32)
                mixed = pltpu.matmul_pop(accs[r * len(pairs) + p])
                mixed = mixed + weights_new[r][p * pair : (p + 1) * pair] * new_value
                for i in range(2):
                    head_rows[pl.ds(r * HQ + p * pair + i * group_size, group_size), :] = mixed[
                        i * group_size : (i + 1) * group_size, i * HD : (i + 1) * HD
                    ]

    pl.run_scoped(
        attend, *[pltpu.ACC(p % 2)((pair, TILE), jnp.float32) for r in range(rows) for p in pairs]
    )
    lines = rows * KVH
    for j in range(group_size):
        own_rows[:, j * HD : (j + 1) * HD] = head_rows[
            pl.ds(j, lines, stride=group_size), :
        ]
    att_slots[0] = own_rows[...].astype(jnp.bfloat16)
    pl.semaphore_wait(barrier, len(peers))

    def gather_ops(slots, send_sem, recv_sem):
        def copy(first, to, count, k, device):
            return pltpu.make_async_remote_copy(
                src_ref=slots.at[pl.ds(first, count)],
                dst_ref=slots.at[pl.ds(to, count)],
                send_sem=send_sem.at[k],
                recv_sem=recv_sem.at[k],
                device_id={"blk": device},
                device_id_type=MESH_IDS,
            )

        x, c, xc = 2 * NZ, NZ, 3 * NZ
        copies = {
            "z1": copy(0, 1, 1, 0, rank_of(1, 0, 0)),
            "z2": copy(0, 2, 1, 1, rank_of(2, 0, 0)),
            "z3": copy(0, 3, 1, 2, rank_of(3, 0, 0)),
            "x0": copy(0, x, 1, 3, x_peer),
            "x1": copy(1, x + 1, 1, 4, x_peer),
            "x2": copy(2, x + 2, 2, 5, x_peer),
            "c0": copy(0, c, 1, 6, core_peer),
            "c1": copy(1, c + 1, 1, 7, core_peer),
            "c2": copy(2, c + 2, 2, 8, core_peer),
            "cx0": copy(x, xc, 1, 9, core_peer),
            "cx1": copy(x + 1, xc + 1, 1, 10, core_peer),
            "cx2": copy(x + 2, xc + 2, 2, 11, core_peer),
        }
        then = {"z1": "x1 c1", "z3": "x2 c2", "x0": "cx0", "x1": "cx1", "x2": "cx2"}

        def begin():
            for name in ("z3", "z2", "z1", "x0", "c0"):
                copies[name].start()

        def act(names):
            for name in names.split():
                copies[name].wait_recv()
                for following in then.get(name, "").split():
                    copies[following].start()

        def finish():
            for each in copies.values():
                each.wait_send()

        return begin, act, finish

    begin, act, finish1 = gather_ops(att_slots, ag1_send, ag1_recv)
    begin()

    for names in ("z1 z2 z3", "x0 x1 x2", "c0 c1 c2", "cx0 cx1 cx2"):
        act(names)
    for q, dx, dc in arrivals:
        wide = att_slots[NZ * (2 * dx + dc) + q].astype(jnp.float32)
        at = pl.ds(pl.multiple_of(rank_of(q, dx, dc) * lines, 8), lines)
        for j in range(group_size):
            att_wide[j, at, :] = wide[:, j * HD : (j + 1) * HD]
    for i in range(4):
        proj_copy(i).wait()

    def project(*accs):
        parts = []
        for g in range(KVH):
            for j in range(0, group_size, 2):
                parts.append(
                    jnp.concatenate(
                        [
                            att_wide[j + i, pl.ds(g, total_rows, stride=KVH), :]
                            for i in range(2)
                        ],
                        axis=1,
                    ).astype(jnp.bfloat16)
                )
        return times_transposed(parts, proj_w, accs)

    acc_types = [pltpu.ACC(unit)((total_rows, TILE), jnp.float32) for unit in range(2)]
    projected = pl.run_scoped(project, *acc_types)
    after = (residual_ref[...].astype(jnp.float32) + projected).astype(jnp.bfloat16)
    wide = after.astype(jnp.float32)
    gain = gain_ref[...].astype(jnp.float32).reshape(1, width)
    act_slots[0] = (wide * gain).astype(jnp.bfloat16)
    begin, act, finish2 = gather_ops(act_slots, ag2_send, ag2_recv)
    begin()
    for t in range(SPARE, SPARE + per_row):
        down_copy(t).start()
    after_ref[...] = after

    folded = wide[:, 0:LANES] * wide[:, 0:LANES]
    for j in range(1, width // LANES):
        part = wide[:, j * LANES : (j + 1) * LANES]
        folded = folded + part * part
    squares[0] = folded

    def square_copy(k):
        slot = (0, 2, 4, 4, 4)[k]
        return pltpu.make_async_remote_copy(
            src_ref=squares.at[slot],
            dst_ref=squares.at[(1, 3, 5, 6, 7)[k]],
            send_sem=square_send.at[k],
            recv_sem=square_recv.at[k],
            device_id={"blk": peers[k]},
            device_id_type=MESH_IDS,
        )

    square_copy(0).start()

    def squares_over_cores():
        square_copy(0).wait_recv()
        squares[2] = squares[0] + squares[1]
        square_copy(1).start()

    def squares_over_x():
        square_copy(1).wait_recv()
        squares[4] = squares[2] + squares[3]
        for k in (2, 3, 4):
            square_copy(k).start()

    def feed_forward(*accs):
        gate_accs, up_accs = accs[0::2], accs[1::2]

        for t, (q, dx, dc) in enumerate(arrivals):
            s = rank_of(q, dx, dc)
            act(awaited.get(t, ""))
            if t == 3:
                squares_over_cores()
            if t == 7:
                squares_over_x()
            gate_copy(t).wait()
            up_copy(t).wait()
            for k in range(width // TILE):
                part = act_slots[NZ * (2 * dx + dc) + q, :, k * TILE : (k + 1) * TILE]
                span = pl.ds(pl.multiple_of(s * width + k * TILE, TILE), TILE)
                for i in range(hidden_width // TILE):
                    step = k * (hidden_width // TILE) + i
                    tall = pl.ds(i * TILE, TILE)
                    for unit, weights in enumerate((gate_w, up_w)):
                        push(weights[tall, span], step, unit)
                        pltpu.matmul_acc_lhs((gate_accs, up_accs)[unit][i], part, step % 2)
        total = squares[4]
        for k in (2, 3, 4):
            square_copy(k).wait_recv()
            total = total + squares[k + 3]
        inverse_rms = lax.rsqrt(
            jnp.sum(total, axis=1, keepdims=True) / (n * width) + epsilon
        )
        hidden = []
        for gate_acc, up_acc in zip(gate_accs, up_accs):
            gate_sum = pltpu.matmul_pop(gate_acc) * inverse_rms
            up_sum = pltpu.matmul_pop(up_acc) * inverse_rms
            hidden.append((gate_sum / (1.0 + jnp.exp(-gate_sum)) * up_sum).astype(jnp.bfloat16))
        return tuple(hidden)

    hidden = pl.run_scoped(feed_forward, *acc_types * (hidden_width // TILE))
    for t in range(SPARE + per_row, n):
        down_copy(t).start()
    def core_copy(t):
        i = t % NZ + t // (2 * NZ) * NZ
        return pltpu.make_async_remote_copy(
            src_ref=rs_send.at[t],
            dst_ref=core_recv.at[i],
            send_sem=own_send.at[t],
            recv_sem=core_sem.at[i],
            device_id={"blk": core_peer},
            device_id_type=MESH_IDS,
        )

    def x_copy(t):
        return pltpu.make_async_remote_copy(
            src_ref=rs_send.at[t],
            dst_ref=x_recv.at[t % NZ],
            send_sem=own_send.at[t],
            recv_sem=x_sem.at[t % NZ],
            device_id={"blk": x_peer},
            device_id_type=MESH_IDS,
        )

    def z_copy(t):
        return pltpu.make_async_remote_copy(
            src_ref=rs_send.at[t],
            dst_ref=z_recv.at[t % NZ],
            send_sem=own_send.at[t],
            recv_sem=z_sem.at[t % NZ],
            device_id={"blk": rank_of(NZ - 1 - t % NZ, 0, 0)},
            device_id_type=MESH_IDS,
        )

    def term(t):
        down_copy(t).wait()
        return pl.run_scoped(
            lambda *accs: times_transposed(hidden, down_place(t), accs), *acc_types
        )

    sends = []
    for t in (0, 1, 2, 4, 3, 5, 8, 6, 9, 7, 10, 11, 12, 13, 14):
        total = term(t)
        group = t // NZ
        if group % 2 == 1:
            core_copy(t - NZ).wait_recv()
            total = total + core_recv[t % NZ + group // 2 * NZ].astype(jnp.float32)
        if group == 3:
            x_copy(t - 2 * NZ).wait_recv()
            total = total + x_recv[t % NZ].astype(jnp.float32)
        rs_send[t] = total.astype(jnp.bfloat16)
        copy = (core_copy, x_copy, core_copy, z_copy)[group](t)
        copy.start()
        sends.append(copy)
    t = n - 1
    total = term(t)
    core_copy(t - NZ).wait_recv()
    total = total + core_recv[2 * NZ - 1].astype(jnp.float32)
    x_copy(t - 2 * NZ).wait_recv()
    total = total + x_recv[NZ - 1].astype(jnp.float32)
    total = total + after_ref[...].astype(jnp.float32)
    for k in range(NZ - 1):
        z_copy(n - NZ + k).wait_recv()
        total = total + z_recv[k].astype(jnp.float32)
    out_ref[...] = total.astype(jnp.bfloat16)
    for copy in sends:
        copy.wait_send()
    finish1()
    finish2()
    for k in range(len(peers)):
        square_copy(k).wait_send()


def hand_over(after_ref, out_ref, after_to, out_to):
    after_to[...] = after_ref[...]
    out_to[...] = out_ref[...]


def fused_shards(
    queries, new_kv, cache_kv, parents, residual, out_proj, norm_gain, w_gate, w_up, w_down
):
    rows = queries.shape[0]
    n = NZ * NX * NC
    width, depth = out_proj.shape
    hidden_width = w_gate.shape[0]
    total_rows = n * rows
    bf16, f32 = jnp.bfloat16, jnp.float32
    in_vmem = pl.BlockSpec(memory_space=pltpu.VMEM)
    outside = pl.BlockSpec(memory_space=pl.ANY)
    dma = pltpu.SemaphoreType.DMA
    after, out = pl.pallas_call(
        functools.partial(fused_kernel, rows),
        out_shape=(
            pltpu.VMEM((total_rows, width), bf16),
            pltpu.VMEM((total_rows, width), bf16),
        ),
        in_specs=[pl.BlockSpec(memory_space=pltpu.SMEM)] + [in_vmem] * 4 + [outside] * 5,
        out_specs=(in_vmem, in_vmem),
        scratch_shapes=[
            pltpu.VMEM((rows, CACHE, KVH * HD), bf16),
            pltpu.VMEM((rows, CACHE, KVH * HD), bf16),
            pltpu.VMEM((width, depth), bf16),
            pltpu.VMEM((hidden_width, depth), bf16),
            pltpu.VMEM((hidden_width, depth), bf16),
            pltpu.VMEM((SPARE, width, hidden_width), bf16),
            pltpu.VMEM((n, rows * KVH, depth // KVH), bf16),
            pltpu.VMEM((HQ // KVH, total_rows * KVH, HD), f32),
            pltpu.VMEM((rows * HQ, HD), f32),
            pltpu.VMEM((rows * KVH, depth // KVH), f32),
            pltpu.VMEM((n, total_rows, width), bf16),
            pltpu.VMEM((8, total_rows, LANES), f32),
            pltpu.VMEM((n - 1, total_rows, width), bf16),
            pltpu.VMEM((NZ * NX, total_rows, width), bf16),
            pltpu.VMEM((NZ, total_rows, width), bf16),
            pltpu.VMEM((NZ - 1, total_rows, width), bf16),
            dma((rows, 2)),
            dma((4,)),
            dma((n,)),
            dma((n,)),
            dma((n,)),
            dma((5,)),
            dma((5,)),
            dma((12,)),
            dma((12,)),
            dma((12,)),
            dma((12,)),
            dma((n - 1,)),
            dma((NZ * NX,)),
            dma((NZ,)),
            dma((NZ - 1,)),
        ],
        compiler_params=pltpu.CompilerParams(
            collective_id=0, has_side_effects=True, vmem_limit_bytes=66800000
        ),
        name="layer",
    )(
        parents,
        queries,
        new_kv,
        norm_gain,
        residual.T,
        cache_kv,
        out_proj,
        w_gate,
        w_up,
        w_down,
    )
    after, out = pl.pallas_call(
        hand_over, out_shape=(jax.ShapeDtypeStruct((total_rows, width), bf16),) * 2, in_specs=[in_vmem] * 2, out_specs=(in_vmem, in_vmem)
    )(pltpu.with_memory_space_constraint(after, pltpu.VMEM), pltpu.with_memory_space_constraint(out, pltpu.VMEM))
    return after.T, out.T


def solution(mesh):
    fits = mesh.shape["blk"] == NZ * NX * NC
    return jax.shard_map(
        fused_shards if fits else shards,
        mesh=mesh,
        in_specs=(
            P(("groups", "blk"), None),
            P(("groups", "blk"), None, None),
            P(("groups", "blk"), None, None, None),
            P(("groups", "blk")),
            P("blk", "groups"),
            P("blk", None),
            P("blk"),
            P("blk", None),
            P("blk", None),
            P(None, "blk"),
        ),
        out_specs=(P("blk", "groups"), P("blk", "groups")),
        check_vma=False,
    )
```

```python
import functools
import math

import jax
import jax.numpy as jnp
from jax import lax
from jax.experimental import pallas as pl
from jax.experimental.pallas import tpu as pltpu
from jax.sharding import PartitionSpec as P

D = 8192
HQ = 64
KVH = 8
HD = 128
CACHE = 256


epsilon = 1e-06


def attend_rows(queries, new_kv, cache_kv, parents):
    row_count = queries.shape[0]
    group_size = HQ // KVH
    local_parent = parents - lax.axis_index("blk") * row_count
    chosen = jnp.broadcast_to(cache_kv[0], cache_kv.shape)
    for i in range(1, row_count):
        here = (local_parent == i)[:, None, None, None]
        chosen = jnp.where(here, cache_kv[i], chosen)
    cache_keys = chosen[:, 0].reshape(row_count, CACHE, KVH, HD)
    cache_values = chosen[:, 1].reshape(row_count, CACHE, KVH, HD)
    new_key = new_kv[:, 0].reshape(row_count, KVH, HD)
    new_value = new_kv[:, 1].reshape(row_count, KVH, HD)
    query_heads = queries.reshape(row_count, KVH, group_size, HD)
    score_scale = 1.0 / math.sqrt(HD)
    score_cache = (
        jnp.einsum("rgjd,rcgd->rgjc", query_heads, cache_keys, preferred_element_type=jnp.float32)
        * score_scale
    )
    score_new = (
        jnp.einsum("rgjd,rgd->rgj", query_heads, new_key, preferred_element_type=jnp.float32)
        * score_scale
    )
    score_top = jnp.maximum(jnp.max(score_cache, axis=-1), score_new)
    expo_cache = jnp.exp(score_cache - score_top[..., None])
    expo_new = jnp.exp(score_new - score_top)
    denom_sum = jnp.sum(expo_cache, axis=-1) + expo_new
    weight_cache = (expo_cache / denom_sum[..., None]).astype(jnp.bfloat16)
    weight_new = (expo_new / denom_sum).astype(jnp.bfloat16)
    mixed_heads = jnp.einsum(
        "rgjc,rcgd->rgjd", weight_cache, cache_values, preferred_element_type=jnp.float32
    )
    mixed_heads = (
        mixed_heads
        + weight_new.astype(jnp.float32)[..., None] * new_value.astype(jnp.float32)[:, :, None, :]
    )
    return mixed_heads.reshape(row_count, HQ * HD).astype(jnp.bfloat16)


def shards(queries, new_kv, cache_kv, parents, residual, out_proj, norm_gain, w_gate, w_up, w_down):
    attended = attend_rows(queries, new_kv, cache_kv, parents)
    projected = lax.dot_general(
        out_proj,
        lax.all_gather(attended, "blk", axis=0, tiled=True),
        (((1,), (1,)), ((), ())),
        preferred_element_type=jnp.float32,
    )
    after_attention = (residual.astype(jnp.float32) + projected).astype(jnp.bfloat16)
    widened = after_attention.astype(jnp.float32)
    gathered, gain_all = (
        lax.all_gather(after_attention, "blk", axis=0, tiled=True),
        lax.all_gather(norm_gain, "blk", axis=0, tiled=True),
    )
    gathered_wide = gathered.astype(jnp.float32)
    inverse_rms = lax.rsqrt(jnp.sum(gathered_wide * gathered_wide, axis=0) / D + epsilon)
    normed_all = (
        gathered_wide * inverse_rms[None, :] * gain_all.astype(jnp.float32)[:, None]
    ).astype(jnp.bfloat16)
    gate_sum = jnp.dot(w_gate, normed_all, preferred_element_type=jnp.float32)
    up_sum = jnp.dot(w_up, normed_all, preferred_element_type=jnp.float32)
    hidden = (jax.nn.silu(gate_sum) * up_sum).astype(jnp.bfloat16)
    ffn_delta = lax.psum_scatter(
        jnp.dot(w_down, hidden, preferred_element_type=jnp.float32),
        "blk",
        scatter_dimension=0,
        tiled=True,
    )
    layer_out = (widened + ffn_delta).astype(jnp.bfloat16)
    return (after_attention, layer_out)


LANES = 128
TILE = 256
NZ, NX, NC = 4, 2, 2
SPARE = 3
MESH_IDS = pl.DeviceIdType.MESH
NT = (((1,), (1,)), ((), ()))


def push(tile, step, unit):
    if (step + unit) % 5 in (0, 2):
        pltpu.matmul_push_rhs(tile, step % 2, unit, transpose=True)
    else:
        pltpu.matmul_push_rhs(tile.T, step % 2, unit)


def times_transposed(parts, weights, accs):
    for k, part in enumerate(parts):
        for unit, acc in enumerate(accs):
            push(weights[unit * TILE : (unit + 1) * TILE, k * TILE : (k + 1) * TILE], k, unit)
            pltpu.matmul_acc_lhs(acc, part, k % 2)
    return jnp.concatenate([pltpu.matmul_pop(acc) for acc in accs], axis=1)


def fused_kernel(
    rows,
    parents_ref,
    queries_ref,
    new_kv_ref,
    gain_ref,
    residual_ref,
    cache_hbm,
    proj_hbm,
    gate_hbm,
    up_hbm,
    down_hbm,
    after_ref,
    out_ref,
    keys,
    values,
    proj_w,
    gate_w,
    up_w,
    down_w,
    att_slots,
    att_wide,
    head_rows,
    own_rows,
    act_slots,
    squares,
    rs_send,
    core_recv,
    x_recv,
    z_recv,
    cache_sem,
    proj_sem,
    gate_sem,
    up_sem,
    down_sem,
    square_send,
    square_recv,
    ag1_send,
    ag1_recv,
    ag2_send,
    ag2_recv,
    own_send,
    core_sem,
    x_sem,
    z_sem,
):
    me = lax.axis_index("blk")
    core = lax.rem(me, NC)
    along_x = lax.rem(lax.div(me, NC), NX)
    along_z = lax.div(me, NC * NX)
    n = NZ * NX * NC
    width = proj_hbm.shape[0]
    hidden_width = gate_hbm.shape[0]
    total_rows = n * rows

    z_places = (
        along_z,
        along_z + 1 - 2 * lax.rem(along_z, 2),
        NZ - 1 - along_z,
        lax.rem(along_z + 2, NZ),
    )

    def pick(values, t):
        chosen = jnp.int32(values[-1])
        for i in range(len(values) - 1):
            chosen = jnp.where(t == i, values[i], chosen)
        return chosen

    def rank_of(q, dx, dc):
        return (
            z_places[q] * (NX * NC)
            + lax.rem(along_x + dx, NX) * NC
            + lax.rem(core + dc, NC)
        )

    x_peer = rank_of(0, 1, 0)
    core_peer = rank_of(0, 0, 1)

    arrivals = [(0, 0, 0), (0, 0, 1), (1, 0, 0), (0, 1, 0), (1, 0, 1), (0, 1, 1)]
    arrivals += [(2, 0, 0), (3, 0, 0), (2, 0, 1), (3, 0, 1), (1, 1, 0), (1, 1, 1)]
    arrivals += [(2, 1, 0), (3, 1, 0), (2, 1, 1), (3, 1, 1)]
    awaited = {1: "c0", 2: "z1", 3: "x0", 4: "c1", 5: "cx0", 6: "z2 z3", 8: "x1 c2", 11: "cx1", 12: "x2", 14: "cx2"}

    def ordered(t):
        return pick([rank_of(*arrival) for arrival in arrivals], t)

    barrier = pltpu.get_barrier_semaphore()
    z_peers = [rank_of(q, 0, 0) for q in range(1, NZ)]
    peers = [core_peer, x_peer] + z_peers
    for peer in peers:
        pl.semaphore_signal(
            barrier, inc=1, device_id={"blk": peer}, device_id_type=MESH_IDS
        )

    def cache_copy(r, i):
        return pltpu.make_async_copy(
            cache_hbm.at[r, i], (keys, values)[i].at[r], cache_sem.at[r, i]
        )

    def proj_copy(i):
        part = proj_hbm.shape[1] // 4
        span = pl.ds(i * part, part)
        return pltpu.make_async_copy(
            proj_hbm.at[:, span], proj_w.at[:, span], proj_sem.at[i]
        )

    def slab(s):
        return pl.ds(pl.multiple_of(s * width, width), width)

    def gate_copy(t):
        span = slab(ordered(t))
        return pltpu.make_async_copy(
            gate_hbm.at[:, span], gate_w.at[:, span], gate_sem.at[t]
        )

    def up_copy(t):
        span = slab(ordered(t))
        return pltpu.make_async_copy(
            up_hbm.at[:, span], up_w.at[:, span], up_sem.at[t]
        )

    per_row = proj_hbm.shape[1] // hidden_width

    def down_place(t):
        if t < SPARE:
            return down_w.at[t]
        t -= SPARE
        if t < per_row:
            return proj_w.at[:, pl.ds(t * hidden_width, hidden_width)]
        t -= per_row
        return gate_w.at[
            pl.ds(t // per_row * width, width),
            pl.ds(t % per_row * hidden_width, hidden_width),
        ]

    def down_owner(t):
        k, group = t % NZ, t // NZ
        return rank_of(NZ - 1 - k, 1 - group // 2, 1 - group % 2)

    def down_copy(t):
        return pltpu.make_async_copy(
            down_hbm.at[slab(down_owner(t)), :], down_place(t), down_sem.at[t]
        )

    for i in range(2):
        for r in range(rows):
            cache_copy(r, i).start()
    for i in range(4):
        proj_copy(i).start()

    def start_weights(t, carry):
        gate_copy(t).start()
        up_copy(t).start()
        return carry

    lax.fori_loop(0, n, start_weights, 0)
    for t in range(SPARE):
        down_copy(t).start()

    query_wide = queries_ref[...].astype(jnp.float32)
    for h in range(HQ):
        head_rows[pl.ds(h, rows, stride=HQ), :] = query_wide[:, h * HD : (h + 1) * HD]
    group_size = HQ // KVH
    pair = 2 * group_size
    own_head = lax.broadcasted_iota(jnp.int32, (pair, TILE), 0) // group_size == (
        lax.broadcasted_iota(jnp.int32, (pair, TILE), 1) // HD
    )
    score_scale = 1.0 / math.sqrt(HD)
    for r in range(rows):
        cache_copy(r, 0).wait()

    pairs = range(KVH // 2)

    def columns(p):
        return slice(p * TILE, (p + 1) * TILE)

    def attend(*accs):
        parents = [lax.rem(parents_ref[r], rows) for r in range(rows)]
        news, weights, weights_new = [], [], []
        for r in range(rows):
            for p in pairs:
                head_block = head_rows[r * HQ + p * pair : r * HQ + (p + 1) * pair, :]
                spread = jnp.where(own_head, jnp.concatenate([head_block] * 2, axis=1), 0.0)
                step = 2 * r + p // 2
                push(keys[parents[r], :, columns(p)], step, p % 2)
                pltpu.matmul_acc_lhs(accs[r * len(pairs) + p], spread.astype(jnp.bfloat16), step % 2)
                new_key = new_kv_ref[r, 0:1, columns(p)].astype(jnp.float32)
                news.append(jnp.sum(spread * new_key, axis=1, keepdims=True))
        for r in range(rows):
            own_accs = accs[r * len(pairs) : (r + 1) * len(pairs)]
            scores = jnp.concatenate([pltpu.matmul_pop(acc) for acc in own_accs], axis=0) * score_scale
            score_new = (
                jnp.concatenate(news[r * len(pairs) : (r + 1) * len(pairs)], axis=0) * score_scale
            )
            top = jnp.maximum(jnp.max(scores, axis=1, keepdims=True), score_new)
            expo = jnp.exp(scores - top)
            expo_new = jnp.exp(score_new - top)
            denom = jnp.sum(expo, axis=1, keepdims=True) + expo_new
            weights.append((expo / denom).astype(jnp.bfloat16))
            weights_new.append((expo_new / denom).astype(jnp.bfloat16).astype(jnp.float32))
        for r in range(rows):
            cache_copy(r, 1).wait()
        for r in range(rows):
            for p in pairs:
                step = 2 * r + p // 2
                pltpu.matmul_push_rhs(values[parents[r], :, columns(p)], step % 2, p % 2)
                pltpu.matmul_acc_lhs(
                    accs[r * len(pairs) + p], weights[r][p * pair : (p + 1) * pair], step % 2
                )
        for r in range(rows):
            for p in pairs:
                new_value = new_kv_ref[r, 1:2, columns(p)].astype(jnp.float32)
                mixed = pltpu.matmul_pop(accs[r * len(pairs) + p])
                mixed = mixed + weights_new[r][p * pair : (p + 1) * pair] * new_value
                for i in range(2):
                    head_rows[pl.ds(r * HQ + p * pair + i * group_size, group_size), :] = mixed[
                        i * group_size : (i + 1) * group_size, i * HD : (i + 1) * HD
                    ]

    pl.run_scoped(
        attend, *[pltpu.ACC(p % 2)((pair, TILE), jnp.float32) for r in range(rows) for p in pairs]
    )
    lines = rows * KVH
    for j in range(group_size):
        own_rows[:, j * HD : (j + 1) * HD] = head_rows[
            pl.ds(j, lines, stride=group_size), :
        ]
    att_slots[0] = own_rows[...].astype(jnp.bfloat16)
    pl.semaphore_wait(barrier, len(peers))

    def gather_ops(slots, send_sem, recv_sem):
        def copy(first, to, count, k, device):
            return pltpu.make_async_remote_copy(
                src_ref=slots.at[pl.ds(first, count)],
                dst_ref=slots.at[pl.ds(to, count)],
                send_sem=send_sem.at[k],
                recv_sem=recv_sem.at[k],
                device_id={"blk": device},
                device_id_type=MESH_IDS,
            )

        x, c, xc = 2 * NZ, NZ, 3 * NZ
        copies = {
            "z1": copy(0, 1, 1, 0, rank_of(1, 0, 0)),
            "z2": copy(0, 2, 1, 1, rank_of(2, 0, 0)),
            "z3": copy(0, 3, 1, 2, rank_of(3, 0, 0)),
            "x0": copy(0, x, 1, 3, x_peer),
            "x1": copy(1, x + 1, 1, 4, x_peer),
            "x2": copy(2, x + 2, 2, 5, x_peer),
            "c0": copy(0, c, 1, 6, core_peer),
            "c1": copy(1, c + 1, 1, 7, core_peer),
            "c2": copy(2, c + 2, 2, 8, core_peer),
            "cx0": copy(x, xc, 1, 9, core_peer),
            "cx1": copy(x + 1, xc + 1, 1, 10, core_peer),
            "cx2": copy(x + 2, xc + 2, 2, 11, core_peer),
        }
        then = {"z1": "x1 c1", "z3": "x2 c2", "x0": "cx0", "x1": "cx1", "x2": "cx2"}

        def begin():
            for name in ("z1", "z3", "z2", "x0", "c0"):
                copies[name].start()

        def act(names):
            for name in names.split():
                copies[name].wait_recv()
                for following in then.get(name, "").split():
                    copies[following].start()

        def finish():
            for each in copies.values():
                each.wait_send()

        return begin, act, finish

    begin, act, finish1 = gather_ops(att_slots, ag1_send, ag1_recv)
    begin()

    for names in ("z1 z2 z3", "x0 x1 x2", "c0 c1 c2", "cx0 cx1 cx2"):
        act(names)
    for q, dx, dc in arrivals:
        wide = att_slots[NZ * (2 * dx + dc) + q].astype(jnp.float32)
        at = pl.ds(pl.multiple_of(rank_of(q, dx, dc) * lines, 8), lines)
        for j in range(group_size):
            att_wide[j, at, :] = wide[:, j * HD : (j + 1) * HD]
    for i in range(4):
        proj_copy(i).wait()

    def project(*accs):
        parts = []
        for g in range(KVH):
            for j in range(0, group_size, 2):
                parts.append(
                    jnp.concatenate(
                        [
                            att_wide[j + i, pl.ds(g, total_rows, stride=KVH), :]
                            for i in range(2)
                        ],
                        axis=1,
                    ).astype(jnp.bfloat16)
                )
        return times_transposed(parts, proj_w, accs)

    acc_types = [pltpu.ACC(unit)((total_rows, TILE), jnp.float32) for unit in range(2)]
    projected = pl.run_scoped(project, *acc_types)
    after = (residual_ref[...].astype(jnp.float32) + projected).astype(jnp.bfloat16)
    wide = after.astype(jnp.float32)
    gain = gain_ref[...].astype(jnp.float32).reshape(1, width)
    act_slots[0] = (wide * gain).astype(jnp.bfloat16)
    begin, act, finish2 = gather_ops(act_slots, ag2_send, ag2_recv)
    begin()
    for t in range(SPARE, SPARE + per_row):
        down_copy(t).start()
    after_ref[...] = after

    folded = wide[:, 0:LANES] * wide[:, 0:LANES]
    for j in range(1, width // LANES):
        part = wide[:, j * LANES : (j + 1) * LANES]
        folded = folded + part * part
    squares[0] = folded

    def square_copy(k):
        slot = (0, 2, 4, 4, 4)[k]
        return pltpu.make_async_remote_copy(
            src_ref=squares.at[slot],
            dst_ref=squares.at[(1, 3, 5, 6, 7)[k]],
            send_sem=square_send.at[k],
            recv_sem=square_recv.at[k],
            device_id={"blk": peers[k]},
            device_id_type=MESH_IDS,
        )

    square_copy(0).start()

    def squares_over_cores():
        square_copy(0).wait_recv()
        squares[2] = squares[0] + squares[1]
        square_copy(1).start()

    def squares_over_x():
        square_copy(1).wait_recv()
        squares[4] = squares[2] + squares[3]
        for k in (2, 3, 4):
            square_copy(k).start()

    def feed_forward(*accs):
        gate_accs, up_accs = accs[0::2], accs[1::2]

        for t, (q, dx, dc) in enumerate(arrivals):
            s = rank_of(q, dx, dc)
            act(awaited.get(t, ""))
            if t == 3:
                squares_over_cores()
            if t == 7:
                squares_over_x()
            gate_copy(t).wait()
            up_copy(t).wait()
            for k in range(width // TILE):
                part = act_slots[NZ * (2 * dx + dc) + q, :, k * TILE : (k + 1) * TILE]
                span = pl.ds(pl.multiple_of(s * width + k * TILE, TILE), TILE)
                for i in range(hidden_width // TILE):
                    step = k * (hidden_width // TILE) + i
                    tall = pl.ds(i * TILE, TILE)
                    for unit, weights in enumerate((gate_w, up_w)):
                        push(weights[tall, span], step, unit)
                        pltpu.matmul_acc_lhs((gate_accs, up_accs)[unit][i], part, step % 2)
        total = squares[4]
        for k in (2, 3, 4):
            square_copy(k).wait_recv()
            total = total + squares[k + 3]
        inverse_rms = lax.rsqrt(
            jnp.sum(total, axis=1, keepdims=True) / (n * width) + epsilon
        )
        hidden = []
        for gate_acc, up_acc in zip(gate_accs, up_accs):
            gate_sum = pltpu.matmul_pop(gate_acc) * inverse_rms
            up_sum = pltpu.matmul_pop(up_acc) * inverse_rms
            hidden.append((gate_sum / (1.0 + jnp.exp(-gate_sum)) * up_sum).astype(jnp.bfloat16))
        return tuple(hidden)

    hidden = pl.run_scoped(feed_forward, *acc_types * (hidden_width // TILE))
    for t in range(SPARE + per_row, n):
        down_copy(t).start()
    def core_copy(t):
        i = t % NZ + t // (2 * NZ) * NZ
        return pltpu.make_async_remote_copy(
            src_ref=rs_send.at[t],
            dst_ref=core_recv.at[i],
            send_sem=own_send.at[t],
            recv_sem=core_sem.at[i],
            device_id={"blk": core_peer},
            device_id_type=MESH_IDS,
        )

    def x_copy(t):
        return pltpu.make_async_remote_copy(
            src_ref=rs_send.at[t],
            dst_ref=x_recv.at[t % NZ],
            send_sem=own_send.at[t],
            recv_sem=x_sem.at[t % NZ],
            device_id={"blk": x_peer},
            device_id_type=MESH_IDS,
        )

    def z_copy(t):
        return pltpu.make_async_remote_copy(
            src_ref=rs_send.at[t],
            dst_ref=z_recv.at[t % NZ],
            send_sem=own_send.at[t],
            recv_sem=z_sem.at[t % NZ],
            device_id={"blk": rank_of(NZ - 1 - t % NZ, 0, 0)},
            device_id_type=MESH_IDS,
        )

    def term(t):
        down_copy(t).wait()
        return pl.run_scoped(
            lambda *accs: times_transposed(hidden, down_place(t), accs), *acc_types
        )

    sends = []
    for t in (0, 1, 2, 4, 3, 5, 8, 6, 9, 7, 10, 11, 12, 13, 14):
        total = term(t)
        group = t // NZ
        if group % 2 == 1:
            core_copy(t - NZ).wait_recv()
            total = total + core_recv[t % NZ + group // 2 * NZ].astype(jnp.float32)
        if group == 3:
            x_copy(t - 2 * NZ).wait_recv()
            total = total + x_recv[t % NZ].astype(jnp.float32)
        rs_send[t] = total.astype(jnp.bfloat16)
        copy = (core_copy, x_copy, core_copy, z_copy)[group](t)
        copy.start()
        sends.append(copy)
    t = n - 1
    total = term(t)
    core_copy(t - NZ).wait_recv()
    total = total + core_recv[2 * NZ - 1].astype(jnp.float32)
    x_copy(t - 2 * NZ).wait_recv()
    total = total + x_recv[NZ - 1].astype(jnp.float32)
    total = total + after_ref[...].astype(jnp.float32)
    for k in range(NZ - 1):
        z_copy(n - NZ + k).wait_recv()
        total = total + z_recv[k].astype(jnp.float32)
    out_ref[...] = total.astype(jnp.bfloat16)
    for copy in sends:
        copy.wait_send()
    finish1()
    finish2()
    for k in range(len(peers)):
        square_copy(k).wait_send()


def hand_over(after_ref, out_ref, after_to, out_to):
    after_to[...] = after_ref[...]
    out_to[...] = out_ref[...]


def fused_shards(
    queries, new_kv, cache_kv, parents, residual, out_proj, norm_gain, w_gate, w_up, w_down
):
    rows = queries.shape[0]
    n = NZ * NX * NC
    width, depth = out_proj.shape
    hidden_width = w_gate.shape[0]
    total_rows = n * rows
    bf16, f32 = jnp.bfloat16, jnp.float32
    in_vmem = pl.BlockSpec(memory_space=pltpu.VMEM)
    outside = pl.BlockSpec(memory_space=pl.ANY)
    dma = pltpu.SemaphoreType.DMA
    after, out = pl.pallas_call(
        functools.partial(fused_kernel, rows),
        out_shape=(
            pltpu.VMEM((total_rows, width), bf16),
            pltpu.VMEM((total_rows, width), bf16),
        ),
        in_specs=[pl.BlockSpec(memory_space=pltpu.SMEM)] + [in_vmem] * 4 + [outside] * 5,
        out_specs=(in_vmem, in_vmem),
        scratch_shapes=[
            pltpu.VMEM((rows, CACHE, KVH * HD), bf16),
            pltpu.VMEM((rows, CACHE, KVH * HD), bf16),
            pltpu.VMEM((width, depth), bf16),
            pltpu.VMEM((hidden_width, depth), bf16),
            pltpu.VMEM((hidden_width, depth), bf16),
            pltpu.VMEM((SPARE, width, hidden_width), bf16),
            pltpu.VMEM((n, rows * KVH, depth // KVH), bf16),
            pltpu.VMEM((HQ // KVH, total_rows * KVH, HD), f32),
            pltpu.VMEM((rows * HQ, HD), f32),
            pltpu.VMEM((rows * KVH, depth // KVH), f32),
            pltpu.VMEM((n, total_rows, width), bf16),
            pltpu.VMEM((8, total_rows, LANES), f32),
            pltpu.VMEM((n - 1, total_rows, width), bf16),
            pltpu.VMEM((NZ * NX, total_rows, width), bf16),
            pltpu.VMEM((NZ, total_rows, width), bf16),
            pltpu.VMEM((NZ - 1, total_rows, width), bf16),
            dma((rows, 2)),
            dma((4,)),
            dma((n,)),
            dma((n,)),
            dma((n,)),
            dma((5,)),
            dma((5,)),
            dma((12,)),
            dma((12,)),
            dma((12,)),
            dma((12,)),
            dma((n - 1,)),
            dma((NZ * NX,)),
            dma((NZ,)),
            dma((NZ - 1,)),
        ],
        compiler_params=pltpu.CompilerParams(
            collective_id=0, has_side_effects=True, vmem_limit_bytes=66800000
        ),
        name="layer",
    )(
        parents,
        queries,
        new_kv,
        norm_gain,
        residual.T,
        cache_kv,
        out_proj,
        w_gate,
        w_up,
        w_down,
    )
    after, out = pl.pallas_call(
        hand_over, out_shape=(jax.ShapeDtypeStruct((total_rows, width), bf16),) * 2, in_specs=[in_vmem] * 2, out_specs=(in_vmem, in_vmem)
    )(pltpu.with_memory_space_constraint(after, pltpu.VMEM), pltpu.with_memory_space_constraint(out, pltpu.VMEM))
    return after.T, out.T


def solution(mesh):
    fits = mesh.shape["blk"] == NZ * NX * NC
    return jax.shard_map(
        fused_shards if fits else shards,
        mesh=mesh,
        in_specs=(
            P(("groups", "blk"), None),
            P(("groups", "blk"), None, None),
            P(("groups", "blk"), None, None, None),
            P(("groups", "blk")),
            P("blk", "groups"),
            P("blk", None),
            P("blk"),
            P("blk", None),
            P("blk", None),
            P(None, "blk"),
        ),
        out_specs=(P("blk", "groups"), P("blk", "groups")),
        check_vma=False,
    )
```

```python
import functools
import math

import jax
import jax.numpy as jnp
from jax import lax
from jax.experimental import pallas as pl
from jax.experimental.pallas import tpu as pltpu
from jax.sharding import PartitionSpec as P

D = 8192
HQ = 64
KVH = 8
HD = 128
CACHE = 256


epsilon = 1e-06


def attend_rows(queries, new_kv, cache_kv, parents):
    row_count = queries.shape[0]
    group_size = HQ // KVH
    local_parent = parents - lax.axis_index("blk") * row_count
    chosen = jnp.broadcast_to(cache_kv[0], cache_kv.shape)
    for i in range(1, row_count):
        here = (local_parent == i)[:, None, None, None]
        chosen = jnp.where(here, cache_kv[i], chosen)
    cache_keys = chosen[:, 0].reshape(row_count, CACHE, KVH, HD)
    cache_values = chosen[:, 1].reshape(row_count, CACHE, KVH, HD)
    new_key = new_kv[:, 0].reshape(row_count, KVH, HD)
    new_value = new_kv[:, 1].reshape(row_count, KVH, HD)
    query_heads = queries.reshape(row_count, KVH, group_size, HD)
    score_scale = 1.0 / math.sqrt(HD)
    score_cache = (
        jnp.einsum("rgjd,rcgd->rgjc", query_heads, cache_keys, preferred_element_type=jnp.float32)
        * score_scale
    )
    score_new = (
        jnp.einsum("rgjd,rgd->rgj", query_heads, new_key, preferred_element_type=jnp.float32)
        * score_scale
    )
    score_top = jnp.maximum(jnp.max(score_cache, axis=-1), score_new)
    expo_cache = jnp.exp(score_cache - score_top[..., None])
    expo_new = jnp.exp(score_new - score_top)
    denom_sum = jnp.sum(expo_cache, axis=-1) + expo_new
    weight_cache = (expo_cache / denom_sum[..., None]).astype(jnp.bfloat16)
    weight_new = (expo_new / denom_sum).astype(jnp.bfloat16)
    mixed_heads = jnp.einsum(
        "rgjc,rcgd->rgjd", weight_cache, cache_values, preferred_element_type=jnp.float32
    )
    mixed_heads = (
        mixed_heads
        + weight_new.astype(jnp.float32)[..., None] * new_value.astype(jnp.float32)[:, :, None, :]
    )
    return mixed_heads.reshape(row_count, HQ * HD).astype(jnp.bfloat16)


def shards(queries, new_kv, cache_kv, parents, residual, out_proj, norm_gain, w_gate, w_up, w_down):
    attended = attend_rows(queries, new_kv, cache_kv, parents)
    projected = lax.dot_general(
        out_proj,
        lax.all_gather(attended, "blk", axis=0, tiled=True),
        (((1,), (1,)), ((), ())),
        preferred_element_type=jnp.float32,
    )
    after_attention = (residual.astype(jnp.float32) + projected).astype(jnp.bfloat16)
    widened = after_attention.astype(jnp.float32)
    gathered, gain_all = (
        lax.all_gather(after_attention, "blk", axis=0, tiled=True),
        lax.all_gather(norm_gain, "blk", axis=0, tiled=True),
    )
    gathered_wide = gathered.astype(jnp.float32)
    inverse_rms = lax.rsqrt(jnp.sum(gathered_wide * gathered_wide, axis=0) / D + epsilon)
    normed_all = (
        gathered_wide * inverse_rms[None, :] * gain_all.astype(jnp.float32)[:, None]
    ).astype(jnp.bfloat16)
    gate_sum = jnp.dot(w_gate, normed_all, preferred_element_type=jnp.float32)
    up_sum = jnp.dot(w_up, normed_all, preferred_element_type=jnp.float32)
    hidden = (jax.nn.silu(gate_sum) * up_sum).astype(jnp.bfloat16)
    ffn_delta = lax.psum_scatter(
        jnp.dot(w_down, hidden, preferred_element_type=jnp.float32),
        "blk",
        scatter_dimension=0,
        tiled=True,
    )
    layer_out = (widened + ffn_delta).astype(jnp.bfloat16)
    return (after_attention, layer_out)


LANES = 128
TILE = 256
NZ, NX, NC = 4, 2, 2
SPARE = 3
MESH_IDS = pl.DeviceIdType.MESH
NT = (((1,), (1,)), ((), ()))


def push(tile, step, unit):
    if (step + unit) % 5 in (0, 2):
        pltpu.matmul_push_rhs(tile, step % 2, unit, transpose=True)
    else:
        pltpu.matmul_push_rhs(tile.T, step % 2, unit)


def times_transposed(parts, weights, accs):
    for k, part in enumerate(parts):
        for unit, acc in enumerate(accs):
            push(weights[unit * TILE : (unit + 1) * TILE, k * TILE : (k + 1) * TILE], k, unit)
            pltpu.matmul_acc_lhs(acc, part, k % 2)
    return jnp.concatenate([pltpu.matmul_pop(acc) for acc in accs], axis=1)


def fused_kernel(
    rows,
    parents_ref,
    queries_ref,
    new_kv_ref,
    gain_ref,
    residual_ref,
    cache_hbm,
    proj_hbm,
    gate_hbm,
    up_hbm,
    down_hbm,
    after_ref,
    out_ref,
    keys,
    values,
    proj_w,
    gate_w,
    up_w,
    down_w,
    att_slots,
    att_wide,
    head_rows,
    own_rows,
    act_slots,
    squares,
    rs_send,
    core_recv,
    x_recv,
    z_recv,
    cache_sem,
    proj_sem,
    gate_sem,
    up_sem,
    down_sem,
    square_send,
    square_recv,
    ag1_send,
    ag1_recv,
    ag2_send,
    ag2_recv,
    own_send,
    core_sem,
    x_sem,
    z_sem,
):
    me = lax.axis_index("blk")
    core = lax.rem(me, NC)
    along_x = lax.rem(lax.div(me, NC), NX)
    along_z = lax.div(me, NC * NX)
    n = NZ * NX * NC
    width = proj_hbm.shape[0]
    hidden_width = gate_hbm.shape[0]
    total_rows = n * rows

    z_places = (
        along_z,
        along_z + 1 - 2 * lax.rem(along_z, 2),
        NZ - 1 - along_z,
        lax.rem(along_z + 2, NZ),
    )

    def pick(values, t):
        chosen = jnp.int32(values[-1])
        for i in range(len(values) - 1):
            chosen = jnp.where(t == i, values[i], chosen)
        return chosen

    def rank_of(q, dx, dc):
        return (
            z_places[q] * (NX * NC)
            + lax.rem(along_x + dx, NX) * NC
            + lax.rem(core + dc, NC)
        )

    x_peer = rank_of(0, 1, 0)
    core_peer = rank_of(0, 0, 1)

    arrivals = [(0, 0, 0), (0, 0, 1), (1, 0, 0), (0, 1, 0), (1, 0, 1), (0, 1, 1)]
    arrivals += [(2, 0, 0), (3, 0, 0), (2, 0, 1), (3, 0, 1), (1, 1, 0), (1, 1, 1)]
    arrivals += [(2, 1, 0), (3, 1, 0), (2, 1, 1), (3, 1, 1)]
    awaited = {1: "c0", 2: "z1", 3: "x0", 4: "c1", 5: "cx0", 6: "z2 z3", 8: "x1 c2", 11: "cx1", 12: "x2 x3", 14: "cx2"}

    def ordered(t):
        return pick([rank_of(*arrival) for arrival in arrivals], t)

    barrier = pltpu.get_barrier_semaphore()
    z_peers = [rank_of(q, 0, 0) for q in range(1, NZ)]
    peers = [core_peer, x_peer] + z_peers
    for peer in peers:
        pl.semaphore_signal(
            barrier, inc=1, device_id={"blk": peer}, device_id_type=MESH_IDS
        )

    def cache_copy(r, i):
        return pltpu.make_async_copy(
            cache_hbm.at[r, i], (keys, values)[i].at[r], cache_sem.at[r, i]
        )

    def proj_copy(i):
        part = proj_hbm.shape[1] // 4
        span = pl.ds(i * part, part)
        return pltpu.make_async_copy(
            proj_hbm.at[:, span], proj_w.at[:, span], proj_sem.at[i]
        )

    def slab(s):
        return pl.ds(pl.multiple_of(s * width, width), width)

    def gate_copy(t):
        span = slab(ordered(t))
        return pltpu.make_async_copy(
            gate_hbm.at[:, span], gate_w.at[:, span], gate_sem.at[t]
        )

    def up_copy(t):
        span = slab(ordered(t))
        return pltpu.make_async_copy(
            up_hbm.at[:, span], up_w.at[:, span], up_sem.at[t]
        )

    per_row = proj_hbm.shape[1] // hidden_width

    def down_place(t):
        if t < SPARE:
            return down_w.at[t]
        t -= SPARE
        if t < per_row:
            return proj_w.at[:, pl.ds(t * hidden_width, hidden_width)]
        t -= per_row
        return gate_w.at[
            pl.ds(t // per_row * width, width),
            pl.ds(t % per_row * hidden_width, hidden_width),
        ]

    def down_owner(t):
        k, group = t % NZ, t // NZ
        return rank_of(NZ - 1 - k, 1 - group // 2, 1 - group % 2)

    def down_copy(t):
        return pltpu.make_async_copy(
            down_hbm.at[slab(down_owner(t)), :], down_place(t), down_sem.at[t]
        )

    for i in range(2):
        for r in range(rows):
            cache_copy(r, i).start()
    for i in range(4):
        proj_copy(i).start()

    def start_weights(t, carry):
        gate_copy(t).start()
        up_copy(t).start()
        return carry

    lax.fori_loop(0, n, start_weights, 0)
    for t in range(SPARE):
        down_copy(t).start()

    query_wide = queries_ref[...].astype(jnp.float32)
    for h in range(HQ):
        head_rows[pl.ds(h, rows, stride=HQ), :] = query_wide[:, h * HD : (h + 1) * HD]
    group_size = HQ // KVH
    pair = 2 * group_size
    own_head = lax.broadcasted_iota(jnp.int32, (pair, TILE), 0) // group_size == (
        lax.broadcasted_iota(jnp.int32, (pair, TILE), 1) // HD
    )
    score_scale = 1.0 / math.sqrt(HD)
    for r in range(rows):
        cache_copy(r, 0).wait()

    pairs = range(KVH // 2)

    def columns(p):
        return slice(p * TILE, (p + 1) * TILE)

    def attend(*accs):
        parents = [lax.rem(parents_ref[r], rows) for r in range(rows)]
        news, weights, weights_new = [], [], []
        for r in range(rows):
            for p in pairs:
                head_block = head_rows[r * HQ + p * pair : r * HQ + (p + 1) * pair, :]
                spread = jnp.where(own_head, jnp.concatenate([head_block] * 2, axis=1), 0.0)
                step = 2 * r + p // 2
                push(keys[parents[r], :, columns(p)], step, p % 2)
                pltpu.matmul_acc_lhs(accs[r * len(pairs) + p], spread.astype(jnp.bfloat16), step % 2)
                new_key = new_kv_ref[r, 0:1, columns(p)].astype(jnp.float32)
                news.append(jnp.sum(spread * new_key, axis=1, keepdims=True))
        for r in range(rows):
            own_accs = accs[r * len(pairs) : (r + 1) * len(pairs)]
            scores = jnp.concatenate([pltpu.matmul_pop(acc) for acc in own_accs], axis=0) * score_scale
            score_new = (
                jnp.concatenate(news[r * len(pairs) : (r + 1) * len(pairs)], axis=0) * score_scale
            )
            top = jnp.maximum(jnp.max(scores, axis=1, keepdims=True), score_new)
            expo = jnp.exp(scores - top)
            expo_new = jnp.exp(score_new - top)
            denom = jnp.sum(expo, axis=1, keepdims=True) + expo_new
            weights.append((expo / denom).astype(jnp.bfloat16))
            weights_new.append((expo_new / denom).astype(jnp.bfloat16).astype(jnp.float32))
        for r in range(rows):
            cache_copy(r, 1).wait()
        for r in range(rows):
            for p in pairs:
                step = 2 * r + p // 2
                pltpu.matmul_push_rhs(values[parents[r], :, columns(p)], step % 2, p % 2)
                pltpu.matmul_acc_lhs(
                    accs[r * len(pairs) + p], weights[r][p * pair : (p + 1) * pair], step % 2
                )
        for r in range(rows):
            for p in pairs:
                new_value = new_kv_ref[r, 1:2, columns(p)].astype(jnp.float32)
                mixed = pltpu.matmul_pop(accs[r * len(pairs) + p])
                mixed = mixed + weights_new[r][p * pair : (p + 1) * pair] * new_value
                for i in range(2):
                    head_rows[pl.ds(r * HQ + p * pair + i * group_size, group_size), :] = mixed[
                        i * group_size : (i + 1) * group_size, i * HD : (i + 1) * HD
                    ]

    pl.run_scoped(
        attend, *[pltpu.ACC(p % 2)((pair, TILE), jnp.float32) for r in range(rows) for p in pairs]
    )
    lines = rows * KVH
    for j in range(group_size):
        own_rows[:, j * HD : (j + 1) * HD] = head_rows[
            pl.ds(j, lines, stride=group_size), :
        ]
    att_slots[0] = own_rows[...].astype(jnp.bfloat16)
    pl.semaphore_wait(barrier, len(peers))

    def gather_ops(slots, send_sem, recv_sem):
        def copy(first, to, count, k, device):
            return pltpu.make_async_remote_copy(
                src_ref=slots.at[pl.ds(first, count)],
                dst_ref=slots.at[pl.ds(to, count)],
                send_sem=send_sem.at[k],
                recv_sem=recv_sem.at[k],
                device_id={"blk": device},
                device_id_type=MESH_IDS,
            )

        x, c, xc = 2 * NZ, NZ, 3 * NZ
        copies = {
            "z1": copy(0, 1, 1, 0, rank_of(1, 0, 0)),
            "z2": copy(0, 2, 1, 1, rank_of(2, 0, 0)),
            "z3": copy(0, 3, 1, 2, rank_of(3, 0, 0)),
            "x0": copy(0, x, 1, 3, x_peer),
            "x1": copy(1, x + 1, 1, 4, x_peer),
            "x2": copy(2, x + 2, 1, 5, x_peer),
            "x3": copy(3, x + 3, 1, 12, x_peer),
            "c0": copy(0, c, 1, 6, core_peer),
            "c1": copy(1, c + 1, 1, 7, core_peer),
            "c2": copy(2, c + 2, 2, 8, core_peer),
            "cx0": copy(x, xc, 1, 9, core_peer),
            "cx1": copy(x + 1, xc + 1, 1, 10, core_peer),
            "cx2": copy(x + 2, xc + 2, 2, 11, core_peer),
        }
        then = {"z1": "x1 c1", "z2": "x2", "z3": "x3 c2", "x0": "cx0", "x1": "cx1", "x3": "cx2"}

        def begin():
            for name in ("z1", "z3", "z2", "x0", "c0"):
                copies[name].start()

        def act(names):
            for name in names.split():
                copies[name].wait_recv()
                for following in then.get(name, "").split():
                    copies[following].start()

        def finish():
            for each in copies.values():
                each.wait_send()

        return begin, act, finish

    begin, act, finish1 = gather_ops(att_slots, ag1_send, ag1_recv)
    begin()

    for names in ("z1 z2 z3", "x0 x1 x2 x3", "c0 c1 c2", "cx0 cx1 cx2"):
        act(names)
    for q, dx, dc in arrivals:
        wide = att_slots[NZ * (2 * dx + dc) + q].astype(jnp.float32)
        at = pl.ds(pl.multiple_of(rank_of(q, dx, dc) * lines, 8), lines)
        for j in range(group_size):
            att_wide[j, at, :] = wide[:, j * HD : (j + 1) * HD]
    for i in range(4):
        proj_copy(i).wait()

    def project(*accs):
        parts = []
        for g in range(KVH):
            for j in range(0, group_size, 2):
                parts.append(
                    jnp.concatenate(
                        [
                            att_wide[j + i, pl.ds(g, total_rows, stride=KVH), :]
                            for i in range(2)
                        ],
                        axis=1,
                    ).astype(jnp.bfloat16)
                )
        return times_transposed(parts, proj_w, accs)

    acc_types = [pltpu.ACC(unit)((total_rows, TILE), jnp.float32) for unit in range(2)]
    projected = pl.run_scoped(project, *acc_types)
    after = (residual_ref[...].astype(jnp.float32) + projected).astype(jnp.bfloat16)
    wide = after.astype(jnp.float32)
    gain = gain_ref[...].astype(jnp.float32).reshape(1, width)
    act_slots[0] = (wide * gain).astype(jnp.bfloat16)
    begin, act, finish2 = gather_ops(act_slots, ag2_send, ag2_recv)
    begin()
    for t in range(SPARE, SPARE + per_row):
        down_copy(t).start()
    after_ref[...] = after

    folded = wide[:, 0:LANES] * wide[:, 0:LANES]
    for j in range(1, width // LANES):
        part = wide[:, j * LANES : (j + 1) * LANES]
        folded = folded + part * part
    squares[0] = folded

    def square_copy(k):
        slot = (0, 2, 4, 4, 4)[k]
        return pltpu.make_async_remote_copy(
            src_ref=squares.at[slot],
            dst_ref=squares.at[(1, 3, 5, 6, 7)[k]],
            send_sem=square_send.at[k],
            recv_sem=square_recv.at[k],
            device_id={"blk": peers[k]},
            device_id_type=MESH_IDS,
        )

    square_copy(0).start()

    def squares_over_cores():
        square_copy(0).wait_recv()
        squares[2] = squares[0] + squares[1]
        square_copy(1).start()

    def squares_over_x():
        square_copy(1).wait_recv()
        squares[4] = squares[2] + squares[3]
        for k in (2, 3, 4):
            square_copy(k).start()

    def feed_forward(*accs):
        gate_accs, up_accs = accs[0::2], accs[1::2]

        for t, (q, dx, dc) in enumerate(arrivals):
            s = rank_of(q, dx, dc)
            act(awaited.get(t, ""))
            if t == 3:
                squares_over_cores()
            if t == 7:
                squares_over_x()
            gate_copy(t).wait()
            up_copy(t).wait()
            for k in range(width // TILE):
                part = act_slots[NZ * (2 * dx + dc) + q, :, k * TILE : (k + 1) * TILE]
                span = pl.ds(pl.multiple_of(s * width + k * TILE, TILE), TILE)
                for i in range(hidden_width // TILE):
                    step = k * (hidden_width // TILE) + i
                    tall = pl.ds(i * TILE, TILE)
                    for unit, weights in enumerate((gate_w, up_w)):
                        push(weights[tall, span], step, unit)
                        pltpu.matmul_acc_lhs((gate_accs, up_accs)[unit][i], part, step % 2)
        total = squares[4]
        for k in (2, 3, 4):
            square_copy(k).wait_recv()
            total = total + squares[k + 3]
        inverse_rms = lax.rsqrt(
            jnp.sum(total, axis=1, keepdims=True) / (n * width) + epsilon
        )
        hidden = []
        for gate_acc, up_acc in zip(gate_accs, up_accs):
            gate_sum = pltpu.matmul_pop(gate_acc) * inverse_rms
            up_sum = pltpu.matmul_pop(up_acc) * inverse_rms
            hidden.append((gate_sum / (1.0 + jnp.exp(-gate_sum)) * up_sum).astype(jnp.bfloat16))
        return tuple(hidden)

    hidden = pl.run_scoped(feed_forward, *acc_types * (hidden_width // TILE))
    for t in range(SPARE + per_row, n):
        down_copy(t).start()
    def core_copy(t):
        i = t % NZ + t // (2 * NZ) * NZ
        return pltpu.make_async_remote_copy(
            src_ref=rs_send.at[t],
            dst_ref=core_recv.at[i],
            send_sem=own_send.at[t],
            recv_sem=core_sem.at[i],
            device_id={"blk": core_peer},
            device_id_type=MESH_IDS,
        )

    def x_copy(t):
        return pltpu.make_async_remote_copy(
            src_ref=rs_send.at[t],
            dst_ref=x_recv.at[t % NZ],
            send_sem=own_send.at[t],
            recv_sem=x_sem.at[t % NZ],
            device_id={"blk": x_peer},
            device_id_type=MESH_IDS,
        )

    def z_copy(t):
        return pltpu.make_async_remote_copy(
            src_ref=rs_send.at[t],
            dst_ref=z_recv.at[t % NZ],
            send_sem=own_send.at[t],
            recv_sem=z_sem.at[t % NZ],
            device_id={"blk": rank_of(NZ - 1 - t % NZ, 0, 0)},
            device_id_type=MESH_IDS,
        )

    def term(t):
        down_copy(t).wait()
        return pl.run_scoped(
            lambda *accs: times_transposed(hidden, down_place(t), accs), *acc_types
        )

    sends = []
    for t in (0, 1, 2, 4, 3, 5, 8, 6, 9, 7, 10, 11, 12, 13, 14):
        total = term(t)
        group = t // NZ
        if group % 2 == 1:
            core_copy(t - NZ).wait_recv()
            total = total + core_recv[t % NZ + group // 2 * NZ].astype(jnp.float32)
        if group == 3:
            x_copy(t - 2 * NZ).wait_recv()
            total = total + x_recv[t % NZ].astype(jnp.float32)
        rs_send[t] = total.astype(jnp.bfloat16)
        copy = (core_copy, x_copy, core_copy, z_copy)[group](t)
        copy.start()
        sends.append(copy)
    t = n - 1
    total = term(t)
    core_copy(t - NZ).wait_recv()
    total = total + core_recv[2 * NZ - 1].astype(jnp.float32)
    x_copy(t - 2 * NZ).wait_recv()
    total = total + x_recv[NZ - 1].astype(jnp.float32)
    total = total + after_ref[...].astype(jnp.float32)
    for k in range(NZ - 1):
        z_copy(n - NZ + k).wait_recv()
        total = total + z_recv[k].astype(jnp.float32)
    out_ref[...] = total.astype(jnp.bfloat16)
    for copy in sends:
        copy.wait_send()
    finish1()
    finish2()
    for k in range(len(peers)):
        square_copy(k).wait_send()


def hand_over(after_ref, out_ref, after_to, out_to):
    after_to[...] = after_ref[...]
    out_to[...] = out_ref[...]


def fused_shards(
    queries, new_kv, cache_kv, parents, residual, out_proj, norm_gain, w_gate, w_up, w_down
):
    rows = queries.shape[0]
    n = NZ * NX * NC
    width, depth = out_proj.shape
    hidden_width = w_gate.shape[0]
    total_rows = n * rows
    bf16, f32 = jnp.bfloat16, jnp.float32
    in_vmem = pl.BlockSpec(memory_space=pltpu.VMEM)
    outside = pl.BlockSpec(memory_space=pl.ANY)
    dma = pltpu.SemaphoreType.DMA
    after, out = pl.pallas_call(
        functools.partial(fused_kernel, rows),
        out_shape=(
            pltpu.VMEM((total_rows, width), bf16),
            pltpu.VMEM((total_rows, width), bf16),
        ),
        in_specs=[pl.BlockSpec(memory_space=pltpu.SMEM)] + [in_vmem] * 4 + [outside] * 5,
        out_specs=(in_vmem, in_vmem),
        scratch_shapes=[
            pltpu.VMEM((rows, CACHE, KVH * HD), bf16),
            pltpu.VMEM((rows, CACHE, KVH * HD), bf16),
            pltpu.VMEM((width, depth), bf16),
            pltpu.VMEM((hidden_width, depth), bf16),
            pltpu.VMEM((hidden_width, depth), bf16),
            pltpu.VMEM((SPARE, width, hidden_width), bf16),
            pltpu.VMEM((n, rows * KVH, depth // KVH), bf16),
            pltpu.VMEM((HQ // KVH, total_rows * KVH, HD), f32),
            pltpu.VMEM((rows * HQ, HD), f32),
            pltpu.VMEM((rows * KVH, depth // KVH), f32),
            pltpu.VMEM((n, total_rows, width), bf16),
            pltpu.VMEM((8, total_rows, LANES), f32),
            pltpu.VMEM((n - 1, total_rows, width), bf16),
            pltpu.VMEM((NZ * NX, total_rows, width), bf16),
            pltpu.VMEM((NZ, total_rows, width), bf16),
            pltpu.VMEM((NZ - 1, total_rows, width), bf16),
            dma((rows, 2)),
            dma((4,)),
            dma((n,)),
            dma((n,)),
            dma((n,)),
            dma((5,)),
            dma((5,)),
            dma((13,)),
            dma((13,)),
            dma((13,)),
            dma((13,)),
            dma((n - 1,)),
            dma((NZ * NX,)),
            dma((NZ,)),
            dma((NZ - 1,)),
        ],
        compiler_params=pltpu.CompilerParams(
            collective_id=0, has_side_effects=True, vmem_limit_bytes=66800000
        ),
        name="layer",
    )(
        parents,
        queries,
        new_kv,
        norm_gain,
        residual.T,
        cache_kv,
        out_proj,
        w_gate,
        w_up,
        w_down,
    )
    after, out = pl.pallas_call(
        hand_over, out_shape=(jax.ShapeDtypeStruct((total_rows, width), bf16),) * 2, in_specs=[in_vmem] * 2, out_specs=(in_vmem, in_vmem)
    )(pltpu.with_memory_space_constraint(after, pltpu.VMEM), pltpu.with_memory_space_constraint(out, pltpu.VMEM))
    return after.T, out.T


def solution(mesh):
    fits = mesh.shape["blk"] == NZ * NX * NC
    return jax.shard_map(
        fused_shards if fits else shards,
        mesh=mesh,
        in_specs=(
            P(("groups", "blk"), None),
            P(("groups", "blk"), None, None),
            P(("groups", "blk"), None, None, None),
            P(("groups", "blk")),
            P("blk", "groups"),
            P("blk", None),
            P("blk"),
            P("blk", None),
            P("blk", None),
            P(None, "blk"),
        ),
        out_specs=(P("blk", "groups"), P("blk", "groups")),
        check_vma=False,
    )
```
